32 devices in a mesh: wa: 8 (over z, x), af: 4 (over y, core).
Axes of the slice: x: 2, y: 2, z: 4, core: 2. Of those that a mesh axis runs over, the one named last changes fastest.
Arguments:
- worker_ids: int32 [131072], P(('wa', 'af')), may hold values from 0 to 32767, as said below
- worker_attrs: bfloat16 [131072, 128], P(('wa', 'af')), may hold values from -16 to 16
- firm_ids: int32 [131072], P(('wa', 'af')), may hold values from 0 to 16383, as said below
- firm_attrs: bfloat16 [131072, 128], P(('wa', 'af')), may hold values from -16 to 16
- affinity: bfloat16 [128, 128], replicated, may hold values from -0.5 to 0.5
Outputs:
- worker_means: float32 [32768, 128], P('wa')
- firm_means: float32 [16384, 128], P('af')
- worker_potential: float32 [32768], P('wa')
- firm_potential: float32 [16384], P('af')
The draws below stay inside these ranges and needn't reach their ends.
Inputs may be any that keep to these rules, and one draw needn't show every extreme that they name: `worker_ids`: type ids come in blocks of 4096 consecutive worker types; in the rows of one device at most 1024 records name one block, and in every device's rows some block is named by exactly 1024. Counts per type are skewed and some types have no record. `firm_ids`: type ids come in blocks of 4096 consecutive firm types; in the rows of one device at most 2048 records name one block, and in every device's rows some block is named by exactly 2048. Counts per type are skewed and some types have no record.
All inputs are finite; a program needn't handle non-finite values.
Results may differ from the reference program's by a relative error of at most 0.00205.
The reference program's roundings to bfloat16 on the way (of `projected`) count: a program that leaves them out, or rounds other values in their place, can miss the bound.
Values may be sent and summed in bfloat16 or wider, within the bound.
A program may use at most 64 MiB of HBM per device.

```python
import math
import jax
import jax.numpy as jnp
from jax import lax

W = 32768
F = 16384
K = 128
R_DEV = 4096
ITERS = 3
WT_DEV = 4096
FT_DEV = 4096
RECORDS = 131072
CAP_W = 1024
CAP_F = 2048


def record_draw(key, salt, n_types, tile_types, capacity):
    key = jax.random.fold_in(key, salt)
    keys = jax.random.split(key, 7)
    groups = n_types // tile_types
    blocks = RECORDS // R_DEV
    heavy = jax.random.randint(keys[0], (blocks, 1), 0, groups)
    column = jnp.arange(R_DEV, dtype=jnp.int32)[None, :]
    spread = jnp.maximum(column - capacity, 0) % (groups - 1)
    owner = jnp.where(column < capacity, heavy, (heavy + 1 + spread) % groups)
    owner = jax.random.permutation(keys[1], owner, axis=1, independent=True)
    first = jax.random.randint(keys[2], (blocks, R_DEV), 0, tile_types)
    second = jax.random.randint(keys[3], (blocks, R_DEV), 0, tile_types)
    offset = jax.random.randint(keys[4], (groups,), 0, tile_types)
    slot = (jnp.minimum(first, second) + offset[owner]) % tile_types
    type_ids = (owner * tile_types + slot).reshape(RECORDS).astype(jnp.int32)
    centers = jax.random.normal(keys[5], (n_types, K), jnp.float32)
    noise = jax.random.normal(keys[6], (RECORDS, K), jnp.float32)
    return (type_ids, centers, noise)


def make_attrs(type_ids, centers, noise):
    scale = 0.5
    return jnp.clip(centers[type_ids] * scale + noise, -16.0, 16.0).astype(jnp.bfloat16)


def draw_worker_ids(key, part):
    type_ids, centers, noise = record_draw(key, 11, W, WT_DEV, CAP_W)
    return type_ids


def draw_worker_attrs(key, part):
    type_ids, centers, noise = record_draw(key, 11, W, WT_DEV, CAP_W)
    return make_attrs(type_ids, centers, noise)


def draw_firm_ids(key, part):
    type_ids, centers, noise = record_draw(key, 12, F, FT_DEV, CAP_F)
    return type_ids


def draw_firm_attrs(key, part):
    type_ids, centers, noise = record_draw(key, 12, F, FT_DEV, CAP_F)
    return make_attrs(type_ids, centers, noise)


def scatter_about(own_key, shape, scale, reach, kind=jnp.bfloat16):
    values = jax.random.normal(own_key, shape, jnp.float32) * scale
    return jnp.minimum(jnp.maximum(values, -reach), reach).astype(kind)


def setup_inputs(seed: int = 0) -> dict:
    key_list = jax.random.split(jax.random.key(seed), 6)
    worker_ids = draw_worker_ids(jax.random.fold_in(key_list[5], 71), 0)
    worker_attrs = draw_worker_attrs(jax.random.fold_in(key_list[5], 71), 0)
    firm_ids = draw_firm_ids(jax.random.fold_in(key_list[5], 71), 0)
    firm_attrs = draw_firm_attrs(jax.random.fold_in(key_list[5], 71), 0)
    affinity = scatter_about(key_list[4], (K, K), K ** -0.5, 0.5)
    return dict(worker_ids=worker_ids, worker_attrs=worker_attrs, firm_ids=firm_ids, firm_attrs=firm_attrs, affinity=affinity)


def type_means(attrs, type_ids, count):
    totals = jax.ops.segment_sum(attrs.astype(jnp.float32), type_ids, num_segments=count)
    tallies = jax.ops.segment_sum(jnp.ones(type_ids.shape, jnp.float32), type_ids, num_segments=count)
    return totals / jnp.maximum(tallies, 1.0)[:, None], tallies


def reference(worker_ids, worker_attrs, firm_ids, firm_attrs, affinity):
    worker_means, worker_tally = type_means(worker_attrs, worker_ids, W)
    firm_means, firm_tally = type_means(firm_attrs, firm_ids, F)
    log_worker = jnp.log(worker_tally + 1.0) - jnp.log(jnp.float32(RECORDS + W))
    log_firm = jnp.log(firm_tally + 1.0) - jnp.log(jnp.float32(RECORDS + F))
    projected = jnp.dot(worker_means.astype(jnp.bfloat16), affinity, preferred_element_type=jnp.float32).astype(jnp.bfloat16)
    projected = lax.optimization_barrier(projected).astype(jnp.float32)
    firm_rows = lax.optimization_barrier(firm_means.astype(jnp.bfloat16)).astype(jnp.float32)
    height = math.gcd(W, 512)
    stacked = projected.reshape(W // height, height, K)

    def surplus(rows_block):
        return jnp.dot(rows_block, firm_rows.T, precision=lax.Precision.HIGHEST, preferred_element_type=jnp.float32)

    firm_potential = jnp.zeros((F,), jnp.float32)
    worker_potential = jnp.zeros((W,), jnp.float32)
    for rounds in range(ITERS):
        def row_lse(rows_block, shift=firm_potential):
            scores = surplus(rows_block) + shift[None, :]
            peak = jnp.max(scores, axis=1)
            return peak + jnp.log(jnp.sum(jnp.exp(scores - peak[:, None]), axis=1))

        worker_potential = log_worker - lax.map(row_lse, stacked).reshape(W)

        def col_step(carry, inputs):
            peak, total = carry
            rows_block, shift_block = inputs
            scores = surplus(rows_block) + shift_block[:, None]
            new_peak = jnp.maximum(peak, jnp.max(scores, axis=0))
            total = total * jnp.exp(peak - new_peak) + jnp.sum(jnp.exp(scores - new_peak[None, :]), axis=0)
            return (new_peak, total), None

        start = (jnp.full((F,), -1e30, jnp.float32), jnp.zeros((F,), jnp.float32))
        (peak, total), unused = lax.scan(col_step, start, (stacked, worker_potential.reshape(W // height, height)))
        firm_potential = log_firm - (peak + jnp.log(total))
    return worker_means, firm_means, worker_potential, firm_potential
```

```python
import functools
import math

import jax
import jax.numpy as jnp
from jax import lax
from jax.experimental import pallas as pl
from jax.experimental.pallas import tpu as pltpu
from jax.sharding import PartitionSpec as P

W = 32768
F = 16384
ITERS = 3
LANES = 128
VMEM_BYTES = 60 * 1024 * 1024
MESH = pl.DeviceIdType.MESH


def select_kernel(chunk, wide, low_ref, sec_ref, attrs_ref, out_ref, rhs_ref):
    rows, width = attrs_ref.shape
    block = out_ref.shape[1]
    step = pl.program_id(0)

    @pl.when(step == 0)
    def _():
        eye = lax.broadcasted_iota(jnp.int32, (LANES, LANES), 0) == lax.broadcasted_iota(
            jnp.int32, (LANES, LANES), 1
        )

        def fill(c, carry):
            sec_row = jnp.broadcast_to(sec_ref[pl.ds(c, 1), :], (LANES, LANES))
            sec_col = jnp.sum(jnp.where(eye, sec_row, 0.0), axis=1, keepdims=True)
            spot = pl.ds(pl.multiple_of(c * LANES, LANES), LANES)
            part = attrs_ref[spot, :].astype(jnp.float32)
            for s in range(wide):
                rhs_ref[spot, s * width : (s + 1) * width] = jnp.where(
                    sec_col == s, part, 0.0
                ).astype(jnp.bfloat16)
            return carry

        lax.fori_loop(0, rows // LANES, fill, 0)

    target = lax.broadcasted_iota(jnp.int32, (block, chunk), 0) + step * block
    total = jnp.zeros((block, wide * width), jnp.float32)
    for c in range(rows // chunk):
        hit = jnp.where(low_ref[c : c + 1, :] == target, 1.0, 0.0).astype(jnp.bfloat16)
        total = total + jnp.dot(
            hit, rhs_ref[c * chunk : (c + 1) * chunk, :], preferred_element_type=jnp.float32
        )
    for s in range(wide):
        out_ref[s] = total[:, s * width : (s + 1) * width].astype(out_ref.dtype)


def select_sum(ids, attrs, count, dtype):
    rows, width = attrs.shape
    wide = 2
    span = count // wide
    block = math.gcd(span, 256)
    chunk = math.gcd(rows, 512)
    sec = ids // span
    low = (ids - sec * span).reshape(rows // chunk, chunk)
    sec = sec.astype(jnp.float32).reshape(rows // LANES, LANES)
    whole = lambda shape: pl.BlockSpec(shape, lambda i: (0,) * len(shape))
    out = pl.pallas_call(
        functools.partial(select_kernel, chunk, wide),
        grid=(span // block,),
        out_shape=jax.ShapeDtypeStruct((wide, span, width), dtype),
        in_specs=[whole(low.shape), whole(sec.shape), whole(attrs.shape)],
        out_specs=pl.BlockSpec((wide, block, width), lambda i: (0, i, 0)),
        scratch_shapes=[pltpu.VMEM((rows, wide * width), jnp.bfloat16)],
        compiler_params=pltpu.CompilerParams(vmem_limit_bytes=VMEM_BYTES),
        cost_estimate=pl.CostEstimate(
            flops=2 * rows * count * width, bytes_accessed=rows * width * 4, transcendentals=0
        ),
        name="select_sum",
    )(low, sec, attrs)
    return out.reshape(count, width)


def pack_records(type_ids, attrs, tile, groups, capacity):
    rows = type_ids.shape[0]
    owner = type_ids // tile
    local = type_ids - owner * tile
    grid = owner.reshape(rows // LANES, LANES)
    hits = (grid[None] == jnp.arange(groups, dtype=jnp.int32)[:, None, None])
    ramp = jnp.arange(LANES, dtype=jnp.int32)
    upper = (ramp[:, None] <= ramp[None, :]).astype(jnp.bfloat16)
    within = jnp.dot(hits.astype(jnp.bfloat16), upper, preferred_element_type=jnp.float32)
    lines = within[:, :, -1]
    line = jnp.arange(rows // LANES, dtype=jnp.int32)
    before = jnp.sum(
        jnp.where(line[None, :, None] < line[None, None, :], lines[:, :, None], 0.0), axis=1
    )
    rank = jnp.sum(jnp.where(hits, within - 1.0 + before[:, :, None], 0.0), axis=0)
    place = (grid * capacity + rank.astype(jnp.int32)).reshape(rows)
    sent_attrs = select_sum(place, attrs, groups * capacity, jnp.bfloat16)
    high, lowd = local // 64, local % 64
    filled = jnp.full((groups * capacity,), tile, jnp.int32)
    chosen = place_ids(place, jnp.stack([high, lowd, jnp.ones_like(high)]), groups, capacity)
    sent_ids = jnp.where(chosen[2] > 0.5, (chosen[0] * 64.0 + chosen[1]).astype(jnp.int32), filled)
    return (sent_attrs.reshape(groups, capacity, attrs.shape[1]), sent_ids.reshape(groups, capacity))


def place_ids(place, digits, groups, capacity):
    slots = groups * capacity
    high, low = place // LANES, place % LANES
    ahead = (high[None, :] == jnp.arange(slots // LANES, dtype=jnp.int32)[:, None])
    behind = (low[None, :] == jnp.arange(LANES, dtype=jnp.int32)[:, None]).astype(jnp.bfloat16)
    out = []
    for d in range(digits.shape[0]):
        left = jnp.where(ahead, digits[d][None, :].astype(jnp.bfloat16), jnp.bfloat16(0))
        out.append(
            lax.dot_general(left, behind, (((1,), (1,)), ((), ())), preferred_element_type=jnp.float32)
        )
    return jnp.stack(out).reshape(digits.shape[0], slots)


def pool_records(recv_attrs, recv_ids, tile):
    width = recv_attrs.shape[2]
    flat_ids = recv_ids.reshape(-1)
    totals = select_sum(flat_ids, recv_attrs.reshape(-1, width), tile, jnp.float32)
    high, low = flat_ids // LANES, flat_ids % LANES
    ahead = (high[None, :] == jnp.arange(tile // LANES, dtype=jnp.int32)[:, None])
    behind = (low[None, :] == jnp.arange(LANES, dtype=jnp.int32)[:, None])
    tallies = lax.dot_general(
        ahead.astype(jnp.bfloat16),
        behind.astype(jnp.bfloat16),
        (((1,), (1,)), ((), ())),
        preferred_element_type=jnp.float32,
    )
    return (totals, tallies.reshape(tile))


def shared_means(sums, tally, axis):
    tile, width = sums.shape
    both = lax.psum(jnp.concatenate([sums, tally.reshape(tile // width, width)], axis=0), axis)
    tally = both[tile:].reshape(tile)
    return (both[:tile] / jnp.maximum(tally, 1.0)[:, None], tally)


def joined(value, axis, combine):
    everything = jax.tree.map(lambda part: lax.all_gather(part, axis), value)
    initial = jax.tree.map(lambda part: part[0], everything)

    def step(k, so_far):
        return combine(so_far, jax.tree.map(lambda part: part[k], everything))

    return lax.fori_loop(1, lax.axis_size(axis), step, initial)


def merge_pair(left, right):
    peak = jnp.maximum(left[0], right[0])
    return (peak, left[1] * jnp.exp(left[0] - peak) + right[1] * jnp.exp(right[0] - peak))


def log_sweeps(projected, firm_rows, log_worker, log_firm):
    worker_tile, firm_tile = projected.shape[0], firm_rows.shape[0]
    height = math.gcd(worker_tile, 512)
    blocks = worker_tile // height

    def surplus(index):
        rows_block = lax.dynamic_slice_in_dim(projected, index * height, height, 0)
        return jnp.dot(rows_block, firm_rows.T, preferred_element_type=jnp.float32)

    def sweep(rounds, carry):
        firm_potential = carry[1]

        def row_stats(index):
            scores = surplus(index) + firm_potential[None, :]
            peak = jnp.max(scores, axis=1)
            return (peak, jnp.sum(jnp.exp(scores - peak[:, None]), axis=1))

        peak, total = lax.map(row_stats, jnp.arange(blocks, dtype=jnp.int32))
        peak, total = joined((peak.reshape(-1), total.reshape(-1)), "af", merge_pair)
        worker_potential = log_worker - (peak + jnp.log(total))

        def col_step(carry, inputs):
            peak, total = carry
            index, shift_block = inputs
            scores = surplus(index) + shift_block[:, None]
            new_peak = jnp.maximum(peak, jnp.max(scores, axis=0))
            total = total * jnp.exp(peak - new_peak) + jnp.sum(
                jnp.exp(scores - new_peak[None, :]), axis=0
            )
            return ((new_peak, total), None)

        start = (
            jnp.full((firm_tile,), -jnp.inf, jnp.float32),
            jnp.zeros((firm_tile,), jnp.float32),
        )
        (peak, total), _ = lax.scan(
            col_step,
            start,
            (jnp.arange(blocks, dtype=jnp.int32), worker_potential.reshape(blocks, height)),
        )
        peak, total = joined((peak, total), "wa", merge_pair)
        return (worker_potential, log_firm - (peak + jnp.log(total)))

    start = (jnp.zeros((worker_tile,), jnp.float32), jnp.zeros((firm_tile,), jnp.float32))
    return lax.fori_loop(0, ITERS, sweep, start)


TINY = 4e-28
LEAST = 1e-25
MOST = 1e30


def sweep_kernel(
    wa_size, af_size, proj_ref, firm_ref, wmass_ref, fmass_ref,
    wsum_ref, fsum_ref, bad_ref,
    e_ref, s_ref, v_ref, u_ref, vb_ref, msg_w, msg_f, msg_b, msg_m, in_w, in_f, in_b, in_m,
    send_w, recv_w, send_f, recv_f, send_b, recv_b, send_m, recv_m,
):
    wa, af = lax.axis_index("wa"), lax.axis_index("af")
    wt, ft = proj_ref.shape[0], firm_ref.shape[1]
    wr, fr = wt // LANES, ft // LANES

    barrier = pltpu.get_barrier_semaphore()
    for d in range(1, af_size):
        pl.semaphore_signal(
            barrier, inc=1, device_id=(wa, lax.rem(af + d, af_size)), device_id_type=MESH
        )
    for d in range(1, wa_size):
        pl.semaphore_signal(
            barrier, inc=1, device_id=(lax.rem(wa + d, wa_size), af), device_id_type=MESH
        )

    eye = lax.broadcasted_iota(jnp.int32, (LANES, LANES), 0) == lax.broadcasted_iota(
        jnp.int32, (LANES, LANES), 1
    )

    def lay(column):
        return jnp.sum(jnp.where(eye, column, 0.0), axis=0, keepdims=True)

    def halves(rows):
        row = jnp.concatenate(rows, axis=1)
        top = row.astype(jnp.bfloat16)
        rest = (row - top.astype(jnp.float32)).astype(jnp.bfloat16)
        return jnp.concatenate([top, rest, jnp.zeros((6, row.shape[1]), jnp.bfloat16)], axis=0)

    def exchange(turn, msg, inbox, send, recv, size, along_af):
        copies = []
        for d in range(1, size):
            if along_af:
                peer = (wa, lax.rem(af + d, size))
            else:
                peer = (lax.rem(wa + d, size), af)
            slot = turn * (size - 1) + d - 1
            copies.append(
                pltpu.make_async_remote_copy(
                    src_ref=msg.at[turn],
                    dst_ref=inbox.at[slot],
                    send_sem=send.at[slot],
                    recv_sem=recv.at[slot],
                    device_id=peer,
                    device_id_type=MESH,
                )
            )
        for copy in copies:
            copy.start()
        return copies

    def finish(copies):
        for copy in copies:
            copy.wait()

    def arrival(turn, msg, inbox, size, me, k):
        d = lax.rem(me - k + size, size)
        slot = turn * (size - 1) + jnp.maximum(d - 1, 0)
        return jnp.where(d == 0, msg[turn], inbox[slot])

    def ordered(turn, msg, inbox, size, me, rows, weights=None):
        total = jnp.zeros((rows, LANES), jnp.float32)
        peak = jnp.zeros((8, LANES), jnp.float32)
        for k in range(size):
            value = arrival(turn, msg, inbox, size, me, k)
            part = value[:rows]
            if weights is not None:
                part = part * weights[k]
            total = total + part
            peak = jnp.maximum(peak, value[rows:])
        return total, peak

    def fill(b, carry):
        spot = pl.ds(pl.multiple_of(b * 256, 256), 256)
        peak = jnp.full((256, LANES), -jnp.inf, jnp.float32)
        for c in range(ft // 512):
            scores = jnp.dot(
                proj_ref[spot, :],
                firm_ref[:, c * 512 : (c + 1) * 512],
                preferred_element_type=jnp.float32,
            )
            s_ref[:, c * 512 : (c + 1) * 512] = scores
            for k in range(4):
                peak = jnp.maximum(peak, scores[:, k * LANES : (k + 1) * LANES])
        peak = jnp.max(peak, axis=1, keepdims=True)
        shift = jnp.broadcast_to(peak, (256, LANES))
        acc = jnp.zeros((256, LANES), jnp.float32)
        for c in range(fr):
            grown = jnp.exp(s_ref[:, c * LANES : (c + 1) * LANES] - shift)
            e_ref[spot, c * LANES : (c + 1) * LANES] = grown.astype(jnp.bfloat16)
            acc = acc + grown
        total = jnp.sum(acc, axis=1, keepdims=True)
        for k in range(2):
            part = slice(k * LANES, (k + 1) * LANES)
            msg_w[0, pl.ds(b * 2 + k, 1), :] = lay(total[part])
            msg_m[0, pl.ds(b * 2 + k, 1), :] = lay(peak[part])
        return carry

    lax.fori_loop(0, wt // 256, fill, 0)
    pl.semaphore_wait(barrier, af_size + wa_size - 2)

    fault = jnp.zeros((8, LANES), jnp.float32)
    infinite = jnp.full((8, LANES), jnp.inf, jnp.float32)

    lead = fr // 4
    group = math.gcd(fr - lead, 4)

    def row_pass(turn, scale):
        vb_ref[...] = v_ref[...].astype(jnp.bfloat16)
        spread = halves([v_ref[c : c + 1, :] for c in range(lead)])

        def block(b, carry):
            spot = pl.ds(pl.multiple_of(b * 256, 256), 256)
            near = lax.dot_general(
                spread,
                e_ref[spot, : lead * LANES],
                (((1,), (1,)), ((), ())),
                preferred_element_type=jnp.float32,
            )
            near = near[0:1] + near[1:2]
            for k in range(2):
                part = pl.ds(pl.multiple_of(b * 256 + k * LANES, LANES), LANES)
                acc = jnp.zeros((LANES, LANES), jnp.float32)
                for c in range(lead, fr, group):
                    terms = [
                        e_ref[part, i * LANES : (i + 1) * LANES] * vb_ref[i : i + 1, :]
                        for i in range(c, c + group)
                    ]
                    while len(terms) > 1:
                        terms = [x + y for x, y in zip(terms[::2], terms[1::2])]
                    acc = acc + terms[0].astype(jnp.float32)
                msg_w[turn, pl.ds(b * 2 + k, 1), :] = near[
                    :, k * LANES : (k + 1) * LANES
                ] + lay(jnp.sum(acc, axis=1, keepdims=True))
            return carry

        lax.fori_loop(0, wt // 256, block, 0)
        msg_w[turn, :wr, :] = msg_w[turn, :wr, :] * scale

    def col_pass(turn):
        high = math.gcd(wt, 1024)
        lines = high // LANES

        def block(b, acc):
            spot = pl.ds(pl.multiple_of(b * high, high), high)
            lhs = halves([u_ref[pl.ds(b * lines + k, 1), :] for k in range(lines)])
            return acc + jnp.dot(lhs, e_ref[spot, :], preferred_element_type=jnp.float32)

        acc = lax.fori_loop(0, wt // high, block, jnp.zeros((8, ft), jnp.float32))
        total = acc[0:1] + acc[1:2]
        for c in range(fr):
            msg_f[turn, c : c + 1, :] = total[:, c * LANES : (c + 1) * LANES]

    def judge(total, peak):
        least = jnp.min(total)
        most = jnp.max(total)
        good = (least > LEAST) & (most < MOST)
        fine = jnp.where(good, least, -1.0)
        return jnp.where(peak * TINY <= fine, 0.0, 1.0)

    for turn in range(ITERS):
        if turn == 0:
            biggest = jnp.ones((8, LANES), jnp.float32)
        else:
            row_pass(turn, scale)
            biggest = jnp.full((8, LANES), jnp.max(v_ref[...]), jnp.float32)
        msg_w[turn, wr:, :] = jnp.where(fault > 0.5, infinite, biggest)
        copies = exchange(turn, msg_w, in_w, send_w, recv_w, af_size, True)
        weights = None
        if turn == 0:
            finish(exchange(0, msg_m, in_m, send_m, recv_m, af_size, True))
            peaks = [arrival(0, msg_m, in_m, af_size, af, k) for k in range(af_size)]
            top = functools.reduce(jnp.maximum, peaks)
            weights = [jnp.exp(p - top) for p in peaks]
            scale = jnp.exp(msg_m[0] - top)
        finish(copies)
        total, peak = ordered(turn, msg_w, in_w, af_size, af, wr, weights)
        fault = judge(total, peak)
        u = wmass_ref[...] / total
        u_ref[...] = u * scale
        if turn == ITERS - 1:
            wsum_ref[...] = jnp.log(total) + top
        col_pass(turn)
        least_u = jnp.full((8, LANES), jnp.min(u), jnp.float32)
        spoiled = (fault > 0.5) | (least_u < 1e-35)
        msg_f[turn, fr:, :] = jnp.where(
            spoiled, infinite, jnp.full((8, LANES), jnp.max(u), jnp.float32)
        )
        finish(exchange(turn, msg_f, in_f, send_f, recv_f, wa_size, False))
        total, peak = ordered(turn, msg_f, in_f, wa_size, wa, fr)
        fault = judge(total, peak)
        v_ref[...] = fmass_ref[...] / total
        if turn == ITERS - 1:
            fsum_ref[...] = jnp.log(total)
    msg_b[0] = fault
    finish(exchange(0, msg_b, in_b, send_b, recv_b, af_size, True))
    for d in range(1, af_size):
        fault = jnp.maximum(fault, in_b[d - 1])
    bad_ref[...] = fault


def fast_sweeps(projected, firm_rows, worker_mass, firm_mass):
    wa_size, af_size = lax.axis_size("wa"), lax.axis_size("af")
    wt, ft = projected.shape[0], firm_rows.shape[0]
    wr, fr = wt // LANES, ft // LANES
    vmem = pl.BlockSpec(memory_space=pltpu.VMEM)
    f32 = jnp.float32
    return pl.pallas_call(
        functools.partial(sweep_kernel, wa_size, af_size),
        out_shape=(
            jax.ShapeDtypeStruct((wr, LANES), f32),
            jax.ShapeDtypeStruct((fr, LANES), f32),
            jax.ShapeDtypeStruct((8, LANES), f32),
        ),
        in_specs=[vmem] * 4,
        out_specs=(vmem, vmem, vmem),
        scratch_shapes=[
            pltpu.VMEM((wt, ft), jnp.bfloat16),
            pltpu.VMEM((256, ft), f32),
            pltpu.VMEM((fr, LANES), f32),
            pltpu.VMEM((wr, LANES), f32),
            pltpu.VMEM((fr, LANES), jnp.bfloat16),
            pltpu.VMEM((ITERS, wr + 8, LANES), f32),
            pltpu.VMEM((ITERS, fr + 8, LANES), f32),
            pltpu.VMEM((1, 8, LANES), f32),
            pltpu.VMEM((1, wr, LANES), f32),
            pltpu.VMEM((ITERS * (af_size - 1), wr + 8, LANES), f32),
            pltpu.VMEM((ITERS * (wa_size - 1), fr + 8, LANES), f32),
            pltpu.VMEM((af_size - 1, 8, LANES), f32),
            pltpu.VMEM((af_size - 1, wr, LANES), f32),
            pltpu.SemaphoreType.DMA((ITERS * (af_size - 1),)),
            pltpu.SemaphoreType.DMA((ITERS * (af_size - 1),)),
            pltpu.SemaphoreType.DMA((ITERS * (wa_size - 1),)),
            pltpu.SemaphoreType.DMA((ITERS * (wa_size - 1),)),
            pltpu.SemaphoreType.DMA((af_size - 1,)),
            pltpu.SemaphoreType.DMA((af_size - 1,)),
            pltpu.SemaphoreType.DMA((af_size - 1,)),
            pltpu.SemaphoreType.DMA((af_size - 1,)),
        ],
        compiler_params=pltpu.CompilerParams(
            collective_id=0, has_side_effects=True, vmem_limit_bytes=VMEM_BYTES
        ),
        name="sweeps",
    )(projected, firm_rows.T, worker_mass.reshape(wr, LANES), firm_mass.reshape(fr, LANES))


def body(worker_ids, worker_attrs, firm_ids, firm_attrs, affinity):
    rows = worker_ids.shape[0]
    wa_count = lax.axis_size("wa")
    af_count = lax.axis_size("af")
    worker_tile = W // wa_count
    firm_tile = F // af_count
    records_all = rows * wa_count * af_count
    sent_attrs, sent_ids = pack_records(
        worker_ids, worker_attrs, worker_tile, wa_count, 2 * rows // wa_count
    )
    recv_attrs = lax.all_to_all(sent_attrs, "wa", split_axis=0, concat_axis=0, tiled=True)
    recv_ids = lax.all_to_all(sent_ids, "wa", split_axis=0, concat_axis=0, tiled=True)
    worker_sum, worker_tally = pool_records(recv_attrs, recv_ids, worker_tile)
    sent_attrs, sent_ids = pack_records(
        firm_ids, firm_attrs, firm_tile, af_count, 2 * rows // af_count
    )
    recv_attrs = lax.all_to_all(sent_attrs, "af", split_axis=0, concat_axis=0, tiled=True)
    recv_ids = lax.all_to_all(sent_ids, "af", split_axis=0, concat_axis=0, tiled=True)
    firm_sum, firm_tally = pool_records(recv_attrs, recv_ids, firm_tile)
    worker_means, worker_tally = shared_means(worker_sum, worker_tally, "af")
    firm_means, firm_tally = shared_means(firm_sum, firm_tally, "wa")
    log_worker = jnp.log(worker_tally + 1.0) - jnp.log(jnp.float32(records_all + W))
    log_firm = jnp.log(firm_tally + 1.0) - jnp.log(jnp.float32(records_all + F))
    projected = jnp.dot(
        worker_means.astype(jnp.bfloat16), affinity, preferred_element_type=jnp.float32
    ).astype(jnp.bfloat16)
    firm_rows = firm_means.astype(jnp.bfloat16)
    worker_total, firm_total, bad = fast_sweeps(
        projected,
        firm_rows,
        (worker_tally + 1.0) / jnp.float32(records_all + W),
        (firm_tally + 1.0) / jnp.float32(records_all + F),
    )
    worker_potential, firm_potential = lax.cond(
        bad[0, 0] > 0.5,
        lambda: log_sweeps(projected, firm_rows, log_worker, log_firm),
        lambda: (
            log_worker - worker_total.reshape(-1),
            log_firm - firm_total.reshape(-1),
        ),
    )
    return (
        worker_means,
        firm_means,
        worker_potential,
        firm_potential,
    )


def solution(mesh):
    placed = (P(("wa", "af")), P(("wa", "af"), None), P(("wa", "af")), P(("wa", "af"), None), P())
    return jax.shard_map(
        body,
        mesh=mesh,
        in_specs=placed,
        out_specs=(P("wa", None), P("af", None), P("wa"), P("af")),
        check_vma=False,
    )
```

```python
import functools
import math

import jax
import jax.numpy as jnp
from jax import lax
from jax.experimental import pallas as pl
from jax.experimental.pallas import tpu as pltpu
from jax.sharding import PartitionSpec as P

W = 32768
F = 16384
ITERS = 3
LANES = 128
VMEM_BYTES = 60 * 1024 * 1024
MESH = pl.DeviceIdType.MESH


def upright(row):
    eye = lax.broadcasted_iota(jnp.int32, (LANES, LANES), 0) == lax.broadcasted_iota(
        jnp.int32, (LANES, LANES), 1
    )
    return jnp.sum(jnp.where(eye, row, 0.0), axis=1, keepdims=True)


def route_kernel(
    wa_size, af_size, cap,
    place_ref, wattrs_ref, wids_ref, fids_ref, fattrs_ref, affinity_ref,
    wmeans_ref, fmeans_ref, proj_ref, frows_ref, wtally_ref, ftally_ref,
    rhs_ref, low_ref, send_ref, inw_ref, idw_ref, inf_ref, idf_ref,
    wsum_ref, fsum_ref, near_w, part_w, far_w, near_f, part_f, far_f,
    send_sem, recv_sem,
):
    wa, af = lax.axis_index("wa"), lax.axis_index("af")
    rows = wattrs_ref.shape[0]
    half = wa_size // 2
    wa_high, af_high = wa_size // 2, af_size // 2
    whole_w, whole_f = wmeans_ref.shape[0], fmeans_ref.shape[0]
    wt, ft = whole_w * af_size, whole_f * wa_size
    wa_top, wa_low = wa // 2, lax.rem(wa, 2)
    af_top, af_low = af // 2, lax.rem(af, 2)
    used = [0]

    def copy(src, dst, where):
        slot = used[0]
        used[0] += 1
        return pltpu.make_async_remote_copy(
            src_ref=src,
            dst_ref=dst,
            send_sem=send_sem.at[slot],
            recv_sem=recv_sem.at[slot],
            device_id=where,
            device_id_type=MESH,
        )

    def wa_peer(high, low):
        return (high * 2 + low, af)

    def af_peer(high, low):
        return (wa, high * 2 + low)

    barrier = pltpu.get_barrier_semaphore()
    for d in range(1, wa_size):
        pl.semaphore_signal(
            barrier, inc=1, device_id=(lax.rem(wa + d, wa_size), af), device_id_type=MESH
        )
    for h in range(1, af_high):
        pl.semaphore_signal(
            barrier, inc=1, device_id=af_peer(lax.rem(af_top + h, af_high), af_low),
            device_id_type=MESH,
        )
    pl.semaphore_signal(barrier, inc=1, device_id=af_peer(af_top, 1 - af_low), device_id_type=MESH)

    def split(ids_at, attrs_at, lines, span):
        def fill(c, carry):
            ids = ids_at(c)
            upper = ids >= span
            low_ref[pl.ds(c, 1), :] = jnp.where(upper, ids - span, ids)
            side = upright(jnp.where(upper, 1.0, 0.0))
            spot = pl.ds(pl.multiple_of(c * LANES, LANES), LANES)
            part = attrs_at(spot).astype(jnp.float32)
            rhs_ref[spot, :LANES] = jnp.where(side < 0.5, part, 0.0).astype(jnp.bfloat16)
            rhs_ref[spot, LANES:] = jnp.where(side > 0.5, part, 0.0).astype(jnp.bfloat16)
            return carry

        lax.fori_loop(0, lines, fill, 0, unroll=2)

    def pick(base, block, lines):
        target = lax.broadcasted_iota(jnp.int32, (block, LANES), 0) + base
        step = math.gcd(lines, 8)
        acc = jnp.zeros((block, 2 * LANES), jnp.float32)
        for c in range(0, lines, step):
            hit = jnp.concatenate(
                [
                    jnp.where(low_ref[k : k + 1, :] == target, 1.0, 0.0).astype(jnp.bfloat16)
                    for k in range(c, c + step)
                ],
                axis=1,
            )
            acc = acc + jnp.dot(
                hit,
                rhs_ref[c * LANES : (c + step) * LANES, :],
                preferred_element_type=jnp.float32,
            )
        return acc

    def pool(ids_at, attrs_at, lines, tile, sums_ref, first):
        span = tile // 2
        split(ids_at, attrs_at, lines, span)
        shards, deep, width = sums_ref.shape
        size = deep - 8
        block = math.gcd(math.gcd(span, 1024), size)
        per = size // block

        def step(b, carry):
            acc = pick(b * block, block, lines)
            for side in range(2):
                index = b + side * (span // block)
                spot = pl.ds(pl.multiple_of(lax.rem(index, per) * block, block), block)
                value = acc[:, side * LANES : (side + 1) * LANES]
                if first:
                    sums_ref[index // per, spot, :] = value
                else:
                    sums_ref[index // per, spot, :] += value
            return carry

        lax.fori_loop(0, span // block, step, 0)
        tall = tile // LANES
        total = jnp.zeros((tall, LANES), jnp.float32)
        group = math.gcd(lines, 8)
        for c in range(0, lines, group):
            ahead, behind = [], []
            for k in range(c, c + group):
                ids = ids_at(k)
                high = lax.shift_right_arithmetic(ids, 7)
                rest = ids & (LANES - 1)
                ahead.append(
                    jnp.where(high == lax.broadcasted_iota(jnp.int32, (tall, LANES), 0), 1.0, 0.0)
                )
                behind.append(
                    jnp.where(rest == lax.broadcasted_iota(jnp.int32, (LANES, LANES), 0), 1.0, 0.0)
                )
            total = total + lax.dot_general(
                jnp.concatenate(ahead, axis=1).astype(jnp.bfloat16),
                jnp.concatenate(behind, axis=1).astype(jnp.bfloat16),
                (((1,), (1,)), ((), ())),
                preferred_element_type=jnp.float32,
            )
        counts = size // LANES
        for k in range(shards):
            line = total[k * counts : (k + 1) * counts]
            if first:
                if counts < 8:
                    sums_ref[k, size:, :] = jnp.zeros((8, LANES), jnp.float32)
                sums_ref[k, size : size + counts, :] = line
            else:
                sums_ref[k, size : size + counts, :] += line

    lines = rows // LANES
    cap_lines = cap // LANES
    block = math.gcd(cap, 1024)

    split(lambda c: place_ref[pl.ds(c, 1), :], lambda spot: wattrs_ref[spot, :], lines, half * cap)
    pl.semaphore_wait(barrier, wa_size - 1 + af_high)

    own_high, own_low = [], []
    for h in range(1, af_high):
        where = af_peer(lax.rem(af_top + h, af_high), af_low)
        own_high.append(
            (
                copy(fattrs_ref, inf_ref.at[2 * h], where),
                copy(fids_ref, idf_ref.at[2 * h], where),
            )
        )
    where = af_peer(af_top, 1 - af_low)
    own_low.append(
        (copy(fattrs_ref, inf_ref.at[1], where), copy(fids_ref, idf_ref.at[1], where))
    )
    for pair in own_high + own_low:
        for c in pair:
            c.start()

    sent = {}
    for i in range(half):
        q = lax.rem(wa + i, half)
        one = lax.rem(q - wa + wa_size, wa_size)
        two = lax.rem(one + half, wa_size)

        def fill_block(b, carry):
            acc = pick(q * cap + b * block, block, lines)
            spot = pl.ds(pl.multiple_of(b * block, block), block)
            send_ref[one, spot, :] = acc[:, :LANES].astype(jnp.bfloat16)
            send_ref[two, spot, :] = acc[:, LANES:].astype(jnp.bfloat16)
            return carry

        lax.fori_loop(0, cap // block, fill_block, 0)
        for d in (i + half, i):
            if d:
                to = lax.rem(wa + d, wa_size)
                sent[d] = (
                    copy(send_ref.at[d], inw_ref.at[d - 1], (to, af)),
                    copy(wids_ref.at[to], idw_ref.at[d - 1], (to, af)),
                )
                for c in sent[d]:
                    c.start()

    base = af * ft

    def take_firm(ids_ref, attrs_ref, first):
        pool(
            lambda c: ids_ref[pl.ds(c, 1), :] - base,
            lambda spot: attrs_ref[spot, :],
            lines, ft, fsum_ref, first,
        )

    take_firm(fids_ref, fattrs_ref, True)
    forwards = []
    for h in range(1, af_high):
        for c in own_high[h - 1]:
            c.wait_recv()
        pair = (
            copy(inf_ref.at[2 * h], inf_ref.at[2 * h + 1], af_peer(af_top, 1 - af_low)),
            copy(idf_ref.at[2 * h], idf_ref.at[2 * h + 1], af_peer(af_top, 1 - af_low)),
        )
        for c in pair:
            c.start()
        forwards.append(pair)
    for c in own_low[0]:
        c.wait_recv()
    take_firm(idf_ref.at[1], inf_ref.at[1], False)
    for h in range(1, af_high):
        take_firm(idf_ref.at[2 * h], inf_ref.at[2 * h], False)
    for h in range(1, af_high):
        for c in forwards[h - 1]:
            c.wait_recv()
        take_firm(idf_ref.at[2 * h + 1], inf_ref.at[2 * h + 1], False)

    def scatter_near(sums_ref, near_ref, high, top, low, peer):
        copies = []
        for h in list(range(1, high)) + [0]:
            shard = lax.rem(top + h, high) * 2 + 1 - low
            copies.append(copy(sums_ref.at[shard], near_ref.at[h], peer(top, 1 - low)))
        for c in copies:
            c.start()
        return copies

    def scatter_far(copies, sums_ref, near_ref, part_ref, far_ref, high, top, low, peer):
        out = []
        for i, h in enumerate(list(range(1, high)) + [0]):
            copies[i].wait_recv()
            shard = lax.rem(top + h, high)
            part_ref[h] = sums_ref[shard * 2 + low] + near_ref[h]
            if h:
                out.append(copy(part_ref.at[h], far_ref.at[h - 1], peer(shard, low)))
                out[-1].start()
        return out

    def scatter_end(copies, part_ref, far_ref, high):
        for h in range(1, high):
            copies[h - 1].wait_recv()
            part_ref[0] += far_ref[h - 1]

    def spread_far(refs, high, top, low, peer):
        copies = [[] for _ in range(high)]
        mine = top * 2 + low
        for ref in refs:
            for h in range(1, high):
                copies[h].append(copy(ref.at[mine], ref.at[mine], peer(lax.rem(top + h, high), low)))
            copies[0].append(copy(ref.at[mine], ref.at[mine], peer(top, 1 - low)))
        for h in list(range(1, high)) + [0]:
            for c in copies[h]:
                c.start()
        return copies

    def spread_near(copies, refs, high, top, low, peer):
        out = []
        for h in range(1, high):
            for c in copies[h]:
                c.wait_recv()
            origin = lax.rem(top - h + high, high) * 2 + low
            for ref in refs:
                out.append(copy(ref.at[origin], ref.at[origin], peer(top, 1 - low)))
                out[-1].start()
        return out

    at_wa = (wa_high, wa_top, wa_low, wa_peer)
    at_af = (af_high, af_top, af_low, af_peer)

    near_firm = scatter_near(fsum_ref, near_f, *at_wa)

    def take_worker(d, first=False):
        if d:
            for c in sent[d]:
                c.wait_recv()
            ids, attrs = idw_ref.at[d - 1], inw_ref.at[d - 1]
        else:
            ids, attrs = wids_ref.at[wa], send_ref.at[0]
        pool(
            lambda c: ids[pl.ds(c, 1), :],
            lambda spot: attrs[spot, :],
            cap_lines, wt, wsum_ref, first,
        )

    order = [0]
    for i in range(half):
        order += [d for d in (i + half, i) if d]
    for n, d in enumerate(order):
        take_worker(d, n == 0)

    near_worker = scatter_near(wsum_ref, near_w, *at_af)
    far_firm = scatter_far(near_firm, fsum_ref, near_f, part_f, far_f, *at_wa)
    far_worker = scatter_far(near_worker, wsum_ref, near_w, part_w, far_w, *at_af)

    def finish_means(part_ref, size, means_ref, emit):
        def step(r, carry):
            tally = upright(part_ref[0, pl.ds(size + r, 1), :])
            spot = pl.ds(pl.multiple_of(r * LANES, LANES), LANES)
            means = part_ref[0, spot, :] / jnp.maximum(tally, 1.0)
            means_ref[spot, :] = means
            emit(spot, means.astype(jnp.bfloat16))
            return carry

        lax.fori_loop(0, size // LANES, step, 0)

    def emit_worker(spot, means):
        proj_ref[af, spot, :] = jnp.dot(
            means, affinity_ref[...], preferred_element_type=jnp.float32
        ).astype(jnp.bfloat16)

    def emit_firm(spot, means):
        frows_ref[wa, spot, :] = means

    scatter_end(far_worker, part_w, far_w, af_high)
    finish_means(part_w, whole_w, wmeans_ref, emit_worker)
    wtally_ref[af] = part_w[0, whole_w:, :]
    worker_far = spread_far((proj_ref, wtally_ref), *at_af)
    scatter_end(far_firm, part_f, far_f, wa_high)
    finish_means(part_f, whole_f, fmeans_ref, emit_firm)
    ftally_ref[wa] = part_f[0, whole_f:, :]
    firm_far = spread_far((frows_ref, ftally_ref), *at_wa)
    worker_near = spread_near(worker_far, (proj_ref, wtally_ref), *at_af)
    firm_near = spread_near(firm_far, (frows_ref, ftally_ref), *at_wa)
    for c in worker_far[0] + firm_far[0] + worker_near + firm_near:
        c.wait_recv()
    done = [c for pair in own_high + own_low + forwards + list(sent.values()) for c in pair]
    done += near_firm + near_worker + far_firm + far_worker + worker_near + firm_near
    done += [c for group in worker_far + firm_far for c in group]
    for c in done:
        c.wait_send()


def route(place, worker_attrs, sent_ids, firm_ids, firm_attrs, affinity, cap):
    wa_size, af_size = lax.axis_size("wa"), lax.axis_size("af")
    rows = worker_attrs.shape[0]
    wt, ft = W // wa_size, F // af_size
    sw, sf = wt // af_size, ft // wa_size
    lines = rows // LANES
    wa_high, af_high = wa_size // 2, af_size // 2
    vmem = pl.BlockSpec(memory_space=pltpu.VMEM)
    f32, bf16, i32 = jnp.float32, jnp.bfloat16, jnp.int32
    copies = 4 * af_high + 2 * (wa_size - 1) + 4 * (wa_high + af_high)
    copies += 4 * (wa_high + af_high)
    return pl.pallas_call(
        functools.partial(route_kernel, wa_size, af_size, cap),
        out_shape=(
            jax.ShapeDtypeStruct((sw, LANES), f32),
            jax.ShapeDtypeStruct((sf, LANES), f32),
            jax.ShapeDtypeStruct((af_size, sw, LANES), bf16),
            jax.ShapeDtypeStruct((wa_size, sf, LANES), bf16),
            jax.ShapeDtypeStruct((af_size, 8, LANES), f32),
            jax.ShapeDtypeStruct((wa_size, 8, LANES), f32),
        ),
        in_specs=[vmem] * 6,
        out_specs=(vmem,) * 6,
        scratch_shapes=[
            pltpu.VMEM((rows, 2 * LANES), bf16),
            pltpu.VMEM((lines, LANES), i32),
            pltpu.VMEM((wa_size, cap, LANES), bf16),
            pltpu.VMEM((wa_size - 1, cap, LANES), bf16),
            pltpu.VMEM((wa_size - 1, cap // LANES, LANES), i32),
            pltpu.VMEM((af_size, rows, LANES), bf16),
            pltpu.VMEM((af_size, lines, LANES), i32),
            pltpu.VMEM((af_size, sw + 8, LANES), f32),
            pltpu.VMEM((wa_size, sf + 8, LANES), f32),
            pltpu.VMEM((af_high, sw + 8, LANES), f32),
            pltpu.VMEM((af_high, sw + 8, LANES), f32),
            pltpu.VMEM((max(af_high - 1, 1), sw + 8, LANES), f32),
            pltpu.VMEM((wa_high, sf + 8, LANES), f32),
            pltpu.VMEM((wa_high, sf + 8, LANES), f32),
            pltpu.VMEM((max(wa_high - 1, 1), sf + 8, LANES), f32),
            pltpu.SemaphoreType.DMA((copies,)),
            pltpu.SemaphoreType.DMA((copies,)),
        ],
        compiler_params=pltpu.CompilerParams(
            collective_id=1, has_side_effects=True, vmem_limit_bytes=VMEM_BYTES
        ),
        name="route",
    )(
        place.reshape(lines, LANES),
        worker_attrs,
        sent_ids.reshape(wa_size, cap // LANES, LANES),
        firm_ids.reshape(lines, LANES),
        firm_attrs,
        affinity,
    )


def pack_records(type_ids, tile, groups, capacity):
    rows = type_ids.shape[0]
    owner = type_ids // tile
    local = type_ids - owner * tile
    grid = owner.reshape(rows // LANES, LANES)
    hits = (grid[None] == jnp.arange(groups, dtype=jnp.int32)[:, None, None])
    ramp = jnp.arange(LANES, dtype=jnp.int32)
    upper = (ramp[:, None] <= ramp[None, :]).astype(jnp.bfloat16)
    within = jnp.dot(hits.astype(jnp.bfloat16), upper, preferred_element_type=jnp.float32)
    lines = within[:, :, -1]
    line = jnp.arange(rows // LANES, dtype=jnp.int32)
    before = jnp.sum(
        jnp.where(line[None, :, None] < line[None, None, :], lines[:, :, None], 0.0), axis=1
    )
    rank = jnp.sum(jnp.where(hits, within - 1.0 + before[:, :, None], 0.0), axis=0)
    place = (grid * capacity + rank.astype(jnp.int32)).reshape(rows)
    high, lowd = local // 64, local % 64
    filled = jnp.full((groups * capacity,), tile, jnp.int32)
    chosen = place_ids(place, jnp.stack([high, lowd, jnp.ones_like(high)]), groups, capacity)
    sent_ids = jnp.where(chosen[2] > 0.5, (chosen[0] * 64.0 + chosen[1]).astype(jnp.int32), filled)
    return (place, sent_ids.reshape(groups, capacity))


def place_ids(place, digits, groups, capacity):
    slots = groups * capacity
    high, low = place // LANES, place % LANES
    ahead = (high[None, :] == jnp.arange(slots // LANES, dtype=jnp.int32)[:, None])
    behind = (low[None, :] == jnp.arange(LANES, dtype=jnp.int32)[:, None]).astype(jnp.bfloat16)
    out = []
    for d in range(digits.shape[0]):
        left = jnp.where(ahead, digits[d][None, :].astype(jnp.bfloat16), jnp.bfloat16(0))
        out.append(
            lax.dot_general(left, behind, (((1,), (1,)), ((), ())), preferred_element_type=jnp.float32)
        )
    return jnp.stack(out).reshape(digits.shape[0], slots)


def joined(value, axis, combine):
    everything = jax.tree.map(lambda part: lax.all_gather(part, axis), value)
    initial = jax.tree.map(lambda part: part[0], everything)

    def step(k, so_far):
        return combine(so_far, jax.tree.map(lambda part: part[k], everything))

    return lax.fori_loop(1, lax.axis_size(axis), step, initial)


def merge_pair(left, right):
    peak = jnp.maximum(left[0], right[0])
    return (peak, left[1] * jnp.exp(left[0] - peak) + right[1] * jnp.exp(right[0] - peak))


def log_sweeps(projected, firm_rows, log_worker, log_firm):
    worker_tile, firm_tile = projected.shape[0], firm_rows.shape[0]
    height = math.gcd(worker_tile, 512)
    blocks = worker_tile // height

    def surplus(index):
        rows_block = lax.dynamic_slice_in_dim(projected, index * height, height, 0)
        return jnp.dot(rows_block, firm_rows.T, preferred_element_type=jnp.float32)

    def sweep(rounds, carry):
        firm_potential = carry[1]

        def row_stats(index):
            scores = surplus(index) + firm_potential[None, :]
            peak = jnp.max(scores, axis=1)
            return (peak, jnp.sum(jnp.exp(scores - peak[:, None]), axis=1))

        peak, total = lax.map(row_stats, jnp.arange(blocks, dtype=jnp.int32))
        peak, total = joined((peak.reshape(-1), total.reshape(-1)), "af", merge_pair)
        worker_potential = log_worker - (peak + jnp.log(total))

        def col_step(carry, inputs):
            peak, total = carry
            index, shift_block = inputs
            scores = surplus(index) + shift_block[:, None]
            new_peak = jnp.maximum(peak, jnp.max(scores, axis=0))
            total = total * jnp.exp(peak - new_peak) + jnp.sum(
                jnp.exp(scores - new_peak[None, :]), axis=0
            )
            return ((new_peak, total), None)

        start = (
            jnp.full((firm_tile,), -jnp.inf, jnp.float32),
            jnp.zeros((firm_tile,), jnp.float32),
        )
        (peak, total), _ = lax.scan(
            col_step,
            start,
            (jnp.arange(blocks, dtype=jnp.int32), worker_potential.reshape(blocks, height)),
        )
        peak, total = joined((peak, total), "wa", merge_pair)
        return (worker_potential, log_firm - (peak + jnp.log(total)))

    start = (jnp.zeros((worker_tile,), jnp.float32), jnp.zeros((firm_tile,), jnp.float32))
    return lax.fori_loop(0, ITERS, sweep, start)


TINY = 4e-28
LEAST = 1e-25
MOST = 1e30


def sweep_kernel(
    wa_size, af_size, proj_ref, firm_ref, wmass_ref, fmass_ref,
    wsum_ref, fsum_ref, bad_ref,
    e_ref, s_ref, v_ref, u_ref, vb_ref, msg_w, msg_f, msg_b, msg_m, in_w, in_f, in_b, in_m,
    send_w, recv_w, send_f, recv_f, send_b, recv_b, send_m, recv_m,
):
    wa, af = lax.axis_index("wa"), lax.axis_index("af")
    wt, ft = proj_ref.shape[0], firm_ref.shape[1]
    wr, fr = wt // LANES, ft // LANES

    barrier = pltpu.get_barrier_semaphore()
    for d in range(1, af_size):
        pl.semaphore_signal(
            barrier, inc=1, device_id=(wa, lax.rem(af + d, af_size)), device_id_type=MESH
        )
    for d in range(1, wa_size):
        pl.semaphore_signal(
            barrier, inc=1, device_id=(lax.rem(wa + d, wa_size), af), device_id_type=MESH
        )

    eye = lax.broadcasted_iota(jnp.int32, (LANES, LANES), 0) == lax.broadcasted_iota(
        jnp.int32, (LANES, LANES), 1
    )

    def lay(column):
        return jnp.sum(jnp.where(eye, column, 0.0), axis=0, keepdims=True)

    def halves(rows):
        row = jnp.concatenate(rows, axis=1)
        top = row.astype(jnp.bfloat16)
        rest = (row - top.astype(jnp.float32)).astype(jnp.bfloat16)
        return jnp.concatenate([top, rest, jnp.zeros((6, row.shape[1]), jnp.bfloat16)], axis=0)

    def exchange(turn, msg, inbox, send, recv, size, along_af):
        copies = []
        for d in range(1, size):
            if along_af:
                peer = (wa, lax.rem(af + d, size))
            else:
                peer = (lax.rem(wa + d, size), af)
            slot = turn * (size - 1) + d - 1
            copies.append(
                pltpu.make_async_remote_copy(
                    src_ref=msg.at[turn],
                    dst_ref=inbox.at[slot],
                    send_sem=send.at[slot],
                    recv_sem=recv.at[slot],
                    device_id=peer,
                    device_id_type=MESH,
                )
            )
        for copy in copies:
            copy.start()
        return copies

    def finish(copies):
        for copy in copies:
            copy.wait()

    def arrival(turn, msg, inbox, size, me, k):
        d = lax.rem(me - k + size, size)
        slot = turn * (size - 1) + jnp.maximum(d - 1, 0)
        return jnp.where(d == 0, msg[turn], inbox[slot])

    def ordered(turn, msg, inbox, size, me, rows, weights=None):
        total = jnp.zeros((rows, LANES), jnp.float32)
        peak = jnp.zeros((8, LANES), jnp.float32)
        for k in range(size):
            value = arrival(turn, msg, inbox, size, me, k)
            part = value[:rows]
            if weights is not None:
                part = part * weights[k]
            total = total + part
            peak = jnp.maximum(peak, value[rows:])
        return total, peak

    def fill(b, carry):
        spot = pl.ds(pl.multiple_of(b * 256, 256), 256)
        peak = jnp.full((256, LANES), -jnp.inf, jnp.float32)
        for c in range(ft // 512):
            scores = jnp.dot(
                proj_ref[spot, :],
                firm_ref[:, c * 512 : (c + 1) * 512],
                preferred_element_type=jnp.float32,
            )
            s_ref[:, c * 512 : (c + 1) * 512] = scores
            for k in range(4):
                peak = jnp.maximum(peak, scores[:, k * LANES : (k + 1) * LANES])
        peak = jnp.max(peak, axis=1, keepdims=True)
        shift = jnp.broadcast_to(peak, (256, LANES))
        acc = jnp.zeros((256, LANES), jnp.float32)
        for c in range(fr):
            grown = jnp.exp(s_ref[:, c * LANES : (c + 1) * LANES] - shift)
            e_ref[spot, c * LANES : (c + 1) * LANES] = grown.astype(jnp.bfloat16)
            acc = acc + grown
        total = jnp.sum(acc, axis=1, keepdims=True)
        for k in range(2):
            part = slice(k * LANES, (k + 1) * LANES)
            msg_w[0, pl.ds(b * 2 + k, 1), :] = lay(total[part])
            msg_m[0, pl.ds(b * 2 + k, 1), :] = lay(peak[part])
        return carry

    lax.fori_loop(0, wt // 256, fill, 0)
    pl.semaphore_wait(barrier, af_size + wa_size - 2)

    fault = jnp.zeros((8, LANES), jnp.float32)
    infinite = jnp.full((8, LANES), jnp.inf, jnp.float32)

    lead = fr // 4
    group = math.gcd(fr - lead, 4)

    def row_pass(turn, scale):
        vb_ref[...] = v_ref[...].astype(jnp.bfloat16)
        spread = halves([v_ref[c : c + 1, :] for c in range(lead)])

        def block(b, carry):
            spot = pl.ds(pl.multiple_of(b * 256, 256), 256)
            near = lax.dot_general(
                spread,
                e_ref[spot, : lead * LANES],
                (((1,), (1,)), ((), ())),
                preferred_element_type=jnp.float32,
            )
            near = near[0:1] + near[1:2]
            for k in range(2):
                part = pl.ds(pl.multiple_of(b * 256 + k * LANES, LANES), LANES)
                acc = jnp.zeros((LANES, LANES), jnp.float32)
                for c in range(lead, fr, group):
                    terms = [
                        e_ref[part, i * LANES : (i + 1) * LANES] * vb_ref[i : i + 1, :]
                        for i in range(c, c + group)
                    ]
                    while len(terms) > 1:
                        terms = [x + y for x, y in zip(terms[::2], terms[1::2])]
                    acc = acc + terms[0].astype(jnp.float32)
                msg_w[turn, pl.ds(b * 2 + k, 1), :] = near[
                    :, k * LANES : (k + 1) * LANES
                ] + lay(jnp.sum(acc, axis=1, keepdims=True))
            return carry

        lax.fori_loop(0, wt // 256, block, 0)
        msg_w[turn, :wr, :] = msg_w[turn, :wr, :] * scale

    def col_pass(turn):
        high = math.gcd(wt, 1024)
        lines = high // LANES

        def block(b, acc):
            spot = pl.ds(pl.multiple_of(b * high, high), high)
            lhs = halves([u_ref[pl.ds(b * lines + k, 1), :] for k in range(lines)])
            return acc + jnp.dot(lhs, e_ref[spot, :], preferred_element_type=jnp.float32)

        acc = lax.fori_loop(0, wt // high, block, jnp.zeros((8, ft), jnp.float32))
        total = acc[0:1] + acc[1:2]
        for c in range(fr):
            msg_f[turn, c : c + 1, :] = total[:, c * LANES : (c + 1) * LANES]

    def judge(total, peak):
        least = jnp.min(total)
        most = jnp.max(total)
        good = (least > LEAST) & (most < MOST)
        fine = jnp.where(good, least, -1.0)
        return jnp.where(peak * TINY <= fine, 0.0, 1.0)

    for turn in range(ITERS):
        if turn == 0:
            biggest = jnp.ones((8, LANES), jnp.float32)
        else:
            row_pass(turn, scale)
            biggest = jnp.full((8, LANES), jnp.max(v_ref[...]), jnp.float32)
        msg_w[turn, wr:, :] = jnp.where(fault > 0.5, infinite, biggest)
        copies = exchange(turn, msg_w, in_w, send_w, recv_w, af_size, True)
        weights = None
        if turn == 0:
            finish(exchange(0, msg_m, in_m, send_m, recv_m, af_size, True))
            peaks = [arrival(0, msg_m, in_m, af_size, af, k) for k in range(af_size)]
            top = functools.reduce(jnp.maximum, peaks)
            weights = [jnp.exp(p - top) for p in peaks]
            scale = jnp.exp(msg_m[0] - top)
        finish(copies)
        total, peak = ordered(turn, msg_w, in_w, af_size, af, wr, weights)
        fault = judge(total, peak)
        u = wmass_ref[...] / total
        u_ref[...] = u * scale
        if turn == ITERS - 1:
            wsum_ref[...] = jnp.log(total) + top
        col_pass(turn)
        least_u = jnp.full((8, LANES), jnp.min(u), jnp.float32)
        spoiled = (fault > 0.5) | (least_u < 1e-35)
        msg_f[turn, fr:, :] = jnp.where(
            spoiled, infinite, jnp.full((8, LANES), jnp.max(u), jnp.float32)
        )
        finish(exchange(turn, msg_f, in_f, send_f, recv_f, wa_size, False))
        total, peak = ordered(turn, msg_f, in_f, wa_size, wa, fr)
        fault = judge(total, peak)
        v_ref[...] = fmass_ref[...] / total
        if turn == ITERS - 1:
            fsum_ref[...] = jnp.log(total)
    msg_b[0] = fault
    finish(exchange(0, msg_b, in_b, send_b, recv_b, af_size, True))
    for d in range(1, af_size):
        fault = jnp.maximum(fault, in_b[d - 1])
    bad_ref[...] = fault


def fast_sweeps(projected, firm_rows, worker_mass, firm_mass):
    wa_size, af_size = lax.axis_size("wa"), lax.axis_size("af")
    wt, ft = projected.shape[0], firm_rows.shape[0]
    wr, fr = wt // LANES, ft // LANES
    vmem = pl.BlockSpec(memory_space=pltpu.VMEM)
    f32 = jnp.float32
    return pl.pallas_call(
        functools.partial(sweep_kernel, wa_size, af_size),
        out_shape=(
            jax.ShapeDtypeStruct((wr, LANES), f32),
            jax.ShapeDtypeStruct((fr, LANES), f32),
            jax.ShapeDtypeStruct((8, LANES), f32),
        ),
        in_specs=[vmem] * 4,
        out_specs=(vmem, vmem, vmem),
        scratch_shapes=[
            pltpu.VMEM((wt, ft), jnp.bfloat16),
            pltpu.VMEM((256, ft), f32),
            pltpu.VMEM((fr, LANES), f32),
            pltpu.VMEM((wr, LANES), f32),
            pltpu.VMEM((fr, LANES), jnp.bfloat16),
            pltpu.VMEM((ITERS, wr + 8, LANES), f32),
            pltpu.VMEM((ITERS, fr + 8, LANES), f32),
            pltpu.VMEM((1, 8, LANES), f32),
            pltpu.VMEM((1, wr, LANES), f32),
            pltpu.VMEM((ITERS * (af_size - 1), wr + 8, LANES), f32),
            pltpu.VMEM((ITERS * (wa_size - 1), fr + 8, LANES), f32),
            pltpu.VMEM((af_size - 1, 8, LANES), f32),
            pltpu.VMEM((af_size - 1, wr, LANES), f32),
            pltpu.SemaphoreType.DMA((ITERS * (af_size - 1),)),
            pltpu.SemaphoreType.DMA((ITERS * (af_size - 1),)),
            pltpu.SemaphoreType.DMA((ITERS * (wa_size - 1),)),
            pltpu.SemaphoreType.DMA((ITERS * (wa_size - 1),)),
            pltpu.SemaphoreType.DMA((af_size - 1,)),
            pltpu.SemaphoreType.DMA((af_size - 1,)),
            pltpu.SemaphoreType.DMA((af_size - 1,)),
            pltpu.SemaphoreType.DMA((af_size - 1,)),
        ],
        compiler_params=pltpu.CompilerParams(
            collective_id=0, has_side_effects=True, vmem_limit_bytes=VMEM_BYTES
        ),
        name="sweeps",
    )(projected, firm_rows.T, worker_mass.reshape(wr, LANES), firm_mass.reshape(fr, LANES))


def body(worker_ids, worker_attrs, firm_ids, firm_attrs, affinity):
    rows = worker_ids.shape[0]
    wa_count = lax.axis_size("wa")
    af_count = lax.axis_size("af")
    worker_tile = W // wa_count
    firm_tile = F // af_count
    records_all = rows * wa_count * af_count
    cap = 2 * rows // wa_count
    place, sent_ids = pack_records(worker_ids, worker_tile, wa_count, cap)
    worker_part, firm_part, projected, firm_rows, worker_tally, firm_tally = route(
        place, worker_attrs, sent_ids, firm_ids, firm_attrs, affinity, cap
    )
    projected = projected.reshape(worker_tile, LANES)
    firm_rows = firm_rows.reshape(firm_tile, LANES)
    worker_tally = worker_tally[:, : worker_part.shape[0] // LANES].reshape(worker_tile)
    firm_tally = firm_tally[:, : firm_part.shape[0] // LANES].reshape(firm_tile)
    worker_means = lax.all_gather(worker_part, "af", axis=0, tiled=True)
    firm_means = lax.all_gather(firm_part, "wa", axis=0, tiled=True)
    log_worker = jnp.log(worker_tally + 1.0) - jnp.log(jnp.float32(records_all + W))
    log_firm = jnp.log(firm_tally + 1.0) - jnp.log(jnp.float32(records_all + F))
    worker_total, firm_total, bad = fast_sweeps(
        projected,
        firm_rows,
        (worker_tally + 1.0) / jnp.float32(records_all + W),
        (firm_tally + 1.0) / jnp.float32(records_all + F),
    )
    worker_potential, firm_potential = lax.cond(
        bad[0, 0] > 0.5,
        lambda: log_sweeps(projected, firm_rows, log_worker, log_firm),
        lambda: (
            log_worker - worker_total.reshape(-1),
            log_firm - firm_total.reshape(-1),
        ),
    )
    return (
        worker_means,
        firm_means,
        worker_potential,
        firm_potential,
    )


def solution(mesh):
    placed = (P(("wa", "af")), P(("wa", "af"), None), P(("wa", "af")), P(("wa", "af"), None), P())
    return jax.shard_map(
        body,
        mesh=mesh,
        in_specs=placed,
        out_specs=(P("wa", None), P("af", None), P("wa"), P("af")),
        check_vma=False,
    )
```

```python
import functools
import math

import jax
import jax.numpy as jnp
from jax import lax
from jax.experimental import pallas as pl
from jax.experimental.pallas import tpu as pltpu
from jax.sharding import PartitionSpec as P

W = 32768
F = 16384
ITERS = 3
LANES = 128
VMEM_BYTES = 60 * 1024 * 1024
MESH = pl.DeviceIdType.MESH


def upright(row):
    eye = lax.broadcasted_iota(jnp.int32, (LANES, LANES), 0) == lax.broadcasted_iota(
        jnp.int32, (LANES, LANES), 1
    )
    return jnp.sum(jnp.where(eye, row, 0.0), axis=1, keepdims=True)


def route_kernel(
    wa_size, af_size, cap,
    place_ref, wattrs_ref, wids_ref, fids_ref, fattrs_ref, affinity_ref,
    wmeans_ref, fmeans_ref, proj_ref, frows_ref, wtally_ref, ftally_ref,
    rhs_ref, low_ref, send_ref, inw_ref, idw_ref, inf_ref, idf_ref,
    wsum_ref, fsum_ref, near_w, part_w, far_w, near_f, part_f, far_f,
    send_sem, recv_sem,
):
    wa, af = lax.axis_index("wa"), lax.axis_index("af")
    rows = wattrs_ref.shape[0]
    half = wa_size // 2
    wa_high, af_high = wa_size // 2, af_size // 2
    whole_w, whole_f = wmeans_ref.shape[0], fmeans_ref.shape[0]
    wt, ft = whole_w * af_size, whole_f * wa_size
    wa_top, wa_low = wa // 2, lax.rem(wa, 2)
    af_top, af_low = af // 2, lax.rem(af, 2)
    used = [0]

    def copy(src, dst, where):
        slot = used[0]
        used[0] += 1
        return pltpu.make_async_remote_copy(
            src_ref=src,
            dst_ref=dst,
            send_sem=send_sem.at[slot],
            recv_sem=recv_sem.at[slot],
            device_id=where,
            device_id_type=MESH,
        )

    def wa_peer(high, low):
        return (high * 2 + low, af)

    def af_peer(high, low):
        return (wa, high * 2 + low)

    barrier = pltpu.get_barrier_semaphore()
    for d in range(1, wa_size):
        pl.semaphore_signal(
            barrier, inc=1, device_id=(lax.rem(wa + d, wa_size), af), device_id_type=MESH
        )
    for h in range(1, af_high):
        pl.semaphore_signal(
            barrier, inc=1, device_id=af_peer(lax.rem(af_top + h, af_high), af_low),
            device_id_type=MESH,
        )
    pl.semaphore_signal(barrier, inc=1, device_id=af_peer(af_top, 1 - af_low), device_id_type=MESH)

    def split(ids_at, attrs_at, lines, span):
        def fill(c, carry):
            ids = ids_at(c)
            upper = ids >= span
            low_ref[pl.ds(c, 1), :] = jnp.where(upper, ids - span, ids)
            side = upright(jnp.where(upper, 1.0, 0.0))
            spot = pl.ds(pl.multiple_of(c * LANES, LANES), LANES)
            part = attrs_at(spot).astype(jnp.float32)
            rhs_ref[spot, :LANES] = jnp.where(side < 0.5, part, 0.0).astype(jnp.bfloat16)
            rhs_ref[spot, LANES:] = jnp.where(side > 0.5, part, 0.0).astype(jnp.bfloat16)
            return carry

        lax.fori_loop(0, lines, fill, 0, unroll=2)

    def pick(base, block, lines):
        target = lax.broadcasted_iota(jnp.int32, (block, LANES), 0) + base
        step = math.gcd(lines, 8)
        acc = jnp.zeros((block, 2 * LANES), jnp.float32)
        for c in range(0, lines, step):
            hit = jnp.concatenate(
                [
                    jnp.where(low_ref[k : k + 1, :] == target, 1.0, 0.0).astype(jnp.bfloat16)
                    for k in range(c, c + step)
                ],
                axis=1,
            )
            acc = acc + jnp.dot(
                hit,
                rhs_ref[c * LANES : (c + step) * LANES, :],
                preferred_element_type=jnp.float32,
            )
        return acc

    def pool(ids_at, attrs_at, lines, tile, sums_ref, first):
        span = tile // 2
        split(ids_at, attrs_at, lines, span)
        shards, deep, width = sums_ref.shape
        size = deep - 8
        block = math.gcd(math.gcd(span, 1024), size)
        per = size // block

        def step(b, carry):
            acc = pick(b * block, block, lines)
            for side in range(2):
                index = b + side * (span // block)
                spot = pl.ds(pl.multiple_of(lax.rem(index, per) * block, block), block)
                value = acc[:, side * LANES : (side + 1) * LANES]
                if first:
                    sums_ref[index // per, spot, :] = value
                else:
                    sums_ref[index // per, spot, :] += value
            return carry

        lax.fori_loop(0, span // block, step, 0)
        tall = tile // LANES
        total = jnp.zeros((tall, LANES), jnp.float32)
        group = math.gcd(lines, 8)
        for c in range(0, lines, group):
            ahead, behind = [], []
            for k in range(c, c + group):
                ids = ids_at(k)
                high = lax.shift_right_arithmetic(ids, 7)
                rest = ids & (LANES - 1)
                ahead.append(
                    jnp.where(high == lax.broadcasted_iota(jnp.int32, (tall, LANES), 0), 1.0, 0.0)
                )
                behind.append(
                    jnp.where(rest == lax.broadcasted_iota(jnp.int32, (LANES, LANES), 0), 1.0, 0.0)
                )
            total = total + lax.dot_general(
                jnp.concatenate(ahead, axis=1).astype(jnp.bfloat16),
                jnp.concatenate(behind, axis=1).astype(jnp.bfloat16),
                (((1,), (1,)), ((), ())),
                preferred_element_type=jnp.float32,
            )
        counts = size // LANES
        for k in range(shards):
            line = total[k * counts : (k + 1) * counts]
            if first:
                if counts < 8:
                    sums_ref[k, size:, :] = jnp.zeros((8, LANES), jnp.float32)
                sums_ref[k, size : size + counts, :] = line
            else:
                sums_ref[k, size : size + counts, :] += line

    lines = rows // LANES
    cap_lines = cap // LANES
    block = math.gcd(cap, 1024)

    split(lambda c: place_ref[pl.ds(c, 1), :], lambda spot: wattrs_ref[spot, :], lines, half * cap)
    pl.semaphore_wait(barrier, wa_size - 1 + af_high)

    own_high, own_low = [], []
    for h in range(1, af_high):
        where = af_peer(lax.rem(af_top + h, af_high), af_low)
        own_high.append(
            (
                copy(fattrs_ref, inf_ref.at[2 * h], where),
                copy(fids_ref, idf_ref.at[2 * h], where),
            )
        )
    where = af_peer(af_top, 1 - af_low)
    own_low.append(
        (copy(fattrs_ref, inf_ref.at[1], where), copy(fids_ref, idf_ref.at[1], where))
    )
    for pair in own_high + own_low:
        for c in pair:
            c.start()

    sent = {}
    for i in range(half):
        q = lax.rem(wa + i, half)
        one = lax.rem(q - wa + wa_size, wa_size)
        two = lax.rem(one + half, wa_size)

        def fill_block(b, carry):
            acc = pick(q * cap + b * block, block, lines)
            spot = pl.ds(pl.multiple_of(b * block, block), block)
            send_ref[one, spot, :] = acc[:, :LANES].astype(jnp.bfloat16)
            send_ref[two, spot, :] = acc[:, LANES:].astype(jnp.bfloat16)
            return carry

        lax.fori_loop(0, cap // block, fill_block, 0)
        for d in (i + half, i):
            if d:
                to = lax.rem(wa + d, wa_size)
                sent[d] = (
                    copy(send_ref.at[d], inw_ref.at[d - 1], (to, af)),
                    copy(wids_ref.at[to], idw_ref.at[d - 1], (to, af)),
                )
                for c in sent[d]:
                    c.start()

    base = af * ft

    def take_firm(ids_ref, attrs_ref, first):
        pool(
            lambda c: ids_ref[pl.ds(c, 1), :] - base,
            lambda spot: attrs_ref[spot, :],
            lines, ft, fsum_ref, first,
        )

    take_firm(fids_ref, fattrs_ref, True)
    forwards = []
    for h in range(1, af_high):
        for c in own_high[h - 1]:
            c.wait_recv()
        pair = (
            copy(inf_ref.at[2 * h], inf_ref.at[2 * h + 1], af_peer(af_top, 1 - af_low)),
            copy(idf_ref.at[2 * h], idf_ref.at[2 * h + 1], af_peer(af_top, 1 - af_low)),
        )
        for c in pair:
            c.start()
        forwards.append(pair)
    for c in own_low[0]:
        c.wait_recv()
    take_firm(idf_ref.at[1], inf_ref.at[1], False)
    for h in range(1, af_high):
        take_firm(idf_ref.at[2 * h], inf_ref.at[2 * h], False)
    for h in range(1, af_high):
        for c in forwards[h - 1]:
            c.wait_recv()
        take_firm(idf_ref.at[2 * h + 1], inf_ref.at[2 * h + 1], False)

    def scatter_near(sums_ref, near_ref, high, top, low, peer):
        copies = []
        for h in list(range(1, high)) + [0]:
            shard = lax.rem(top + h, high) * 2 + 1 - low
            copies.append(copy(sums_ref.at[shard], near_ref.at[h], peer(top, 1 - low)))
        for c in copies:
            c.start()
        return copies

    def scatter_far(i, copies, out, sums_ref, near_ref, part_ref, far_ref, high, top, low, peer):
        h = (i + 1) % high
        copies[i].wait_recv()
        shard = lax.rem(top + h, high)
        part_ref[h] = sums_ref[shard * 2 + low] + near_ref[h]
        if h:
            out.append(copy(part_ref.at[h], far_ref.at[h - 1], peer(shard, low)))
            out[-1].start()

    def scatter_end(copies, part_ref, far_ref, high):
        for h in range(1, high):
            copies[h - 1].wait_recv()
            part_ref[0] += far_ref[h - 1]

    def spread_far(refs, high, top, low, peer):
        copies = [[] for _ in range(high)]
        mine = top * 2 + low
        for ref in refs:
            for h in range(1, high):
                copies[h].append(copy(ref.at[mine], ref.at[mine], peer(lax.rem(top + h, high), low)))
            copies[0].append(copy(ref.at[mine], ref.at[mine], peer(top, 1 - low)))
        for h in list(range(1, high)) + [0]:
            for c in copies[h]:
                c.start()
        return copies

    def spread_near(copies, refs, high, top, low, peer):
        out = []
        for h in range(1, high):
            for c in copies[h]:
                c.wait_recv()
            origin = lax.rem(top - h + high, high) * 2 + low
            for ref in refs:
                out.append(copy(ref.at[origin], ref.at[origin], peer(top, 1 - low)))
                out[-1].start()
        return out

    at_wa = (wa_high, wa_top, wa_low, wa_peer)
    at_af = (af_high, af_top, af_low, af_peer)

    near_firm = scatter_near(fsum_ref, near_f, *at_wa)

    def take_worker(d, first=False):
        if d:
            for c in sent[d]:
                c.wait_recv()
            ids, attrs = idw_ref.at[d - 1], inw_ref.at[d - 1]
        else:
            ids, attrs = wids_ref.at[wa], send_ref.at[0]
        pool(
            lambda c: ids[pl.ds(c, 1), :],
            lambda spot: attrs[spot, :],
            cap_lines, wt, wsum_ref, first,
        )

    order = [0]
    for i in range(half):
        order += [d for d in (i + half, i) if d]
    far_firm, far_worker, step = [], [], 0
    for n, d in enumerate(order):
        take_worker(d, n == 0)
        if n >= 2 and n % 2 == 0 and step < wa_high - 1:
            scatter_far(step, near_firm, far_firm, fsum_ref, near_f, part_f, far_f, *at_wa)
            step += 1

    near_worker = scatter_near(wsum_ref, near_w, *at_af)
    for i in range(step, wa_high):
        scatter_far(i, near_firm, far_firm, fsum_ref, near_f, part_f, far_f, *at_wa)
    for i in range(af_high):
        scatter_far(i, near_worker, far_worker, wsum_ref, near_w, part_w, far_w, *at_af)

    def finish_means(part_ref, size, means_ref, emit):
        def step(r, carry):
            tally = upright(part_ref[0, pl.ds(size + r, 1), :])
            spot = pl.ds(pl.multiple_of(r * LANES, LANES), LANES)
            means = part_ref[0, spot, :] / jnp.maximum(tally, 1.0)
            means_ref[spot, :] = means
            emit(spot, means.astype(jnp.bfloat16))
            return carry

        lax.fori_loop(0, size // LANES, step, 0)

    def emit_worker(spot, means):
        proj_ref[af, spot, :] = jnp.dot(
            means, affinity_ref[...], preferred_element_type=jnp.float32
        ).astype(jnp.bfloat16)

    def emit_firm(spot, means):
        frows_ref[wa, spot, :] = means

    scatter_end(far_worker, part_w, far_w, af_high)
    finish_means(part_w, whole_w, wmeans_ref, emit_worker)
    wtally_ref[af] = part_w[0, whole_w:, :]
    worker_far = spread_far((proj_ref, wtally_ref), *at_af)
    scatter_end(far_firm, part_f, far_f, wa_high)
    finish_means(part_f, whole_f, fmeans_ref, emit_firm)
    ftally_ref[wa] = part_f[0, whole_f:, :]
    firm_far = spread_far((frows_ref, ftally_ref), *at_wa)
    worker_near = spread_near(worker_far, (proj_ref, wtally_ref), *at_af)
    firm_near = spread_near(firm_far, (frows_ref, ftally_ref), *at_wa)
    for c in worker_far[0] + firm_far[0] + worker_near + firm_near:
        c.wait_recv()
    done = [c for pair in own_high + own_low + forwards + list(sent.values()) for c in pair]
    done += near_firm + near_worker + far_firm + far_worker + worker_near + firm_near
    done += [c for group in worker_far + firm_far for c in group]
    for c in done:
        c.wait_send()


def route(place, worker_attrs, sent_ids, firm_ids, firm_attrs, affinity, cap):
    wa_size, af_size = lax.axis_size("wa"), lax.axis_size("af")
    rows = worker_attrs.shape[0]
    wt, ft = W // wa_size, F // af_size
    sw, sf = wt // af_size, ft // wa_size
    lines = rows // LANES
    wa_high, af_high = wa_size // 2, af_size // 2
    vmem = pl.BlockSpec(memory_space=pltpu.VMEM)
    f32, bf16, i32 = jnp.float32, jnp.bfloat16, jnp.int32
    copies = 4 * af_high + 2 * (wa_size - 1) + 4 * (wa_high + af_high)
    copies += 4 * (wa_high + af_high)
    return pl.pallas_call(
        functools.partial(route_kernel, wa_size, af_size, cap),
        out_shape=(
            jax.ShapeDtypeStruct((sw, LANES), f32),
            jax.ShapeDtypeStruct((sf, LANES), f32),
            jax.ShapeDtypeStruct((af_size, sw, LANES), bf16),
            jax.ShapeDtypeStruct((wa_size, sf, LANES), bf16),
            jax.ShapeDtypeStruct((af_size, 8, LANES), f32),
            jax.ShapeDtypeStruct((wa_size, 8, LANES), f32),
        ),
        in_specs=[vmem] * 6,
        out_specs=(vmem,) * 6,
        scratch_shapes=[
            pltpu.VMEM((rows, 2 * LANES), bf16),
            pltpu.VMEM((lines, LANES), i32),
            pltpu.VMEM((wa_size, cap, LANES), bf16),
            pltpu.VMEM((wa_size - 1, cap, LANES), bf16),
            pltpu.VMEM((wa_size - 1, cap // LANES, LANES), i32),
            pltpu.VMEM((af_size, rows, LANES), bf16),
            pltpu.VMEM((af_size, lines, LANES), i32),
            pltpu.VMEM((af_size, sw + 8, LANES), f32),
            pltpu.VMEM((wa_size, sf + 8, LANES), f32),
            pltpu.VMEM((af_high, sw + 8, LANES), f32),
            pltpu.VMEM((af_high, sw + 8, LANES), f32),
            pltpu.VMEM((max(af_high - 1, 1), sw + 8, LANES), f32),
            pltpu.VMEM((wa_high, sf + 8, LANES), f32),
            pltpu.VMEM((wa_high, sf + 8, LANES), f32),
            pltpu.VMEM((max(wa_high - 1, 1), sf + 8, LANES), f32),
            pltpu.SemaphoreType.DMA((copies,)),
            pltpu.SemaphoreType.DMA((copies,)),
        ],
        compiler_params=pltpu.CompilerParams(
            collective_id=1, has_side_effects=True, vmem_limit_bytes=VMEM_BYTES
        ),
        name="route",
    )(
        place.reshape(lines, LANES),
        worker_attrs,
        sent_ids.reshape(wa_size, cap // LANES, LANES),
        firm_ids.reshape(lines, LANES),
        firm_attrs,
        affinity,
    )


def pack_records(type_ids, tile, groups, capacity):
    rows = type_ids.shape[0]
    owner = type_ids // tile
    local = type_ids - owner * tile
    grid = owner.reshape(rows // LANES, LANES)
    hits = (grid[None] == jnp.arange(groups, dtype=jnp.int32)[:, None, None])
    ramp = jnp.arange(LANES, dtype=jnp.int32)
    upper = (ramp[:, None] <= ramp[None, :]).astype(jnp.bfloat16)
    within = jnp.dot(hits.astype(jnp.bfloat16), upper, preferred_element_type=jnp.float32)
    lines = within[:, :, -1]
    line = jnp.arange(rows // LANES, dtype=jnp.int32)
    before = jnp.sum(
        jnp.where(line[None, :, None] < line[None, None, :], lines[:, :, None], 0.0), axis=1
    )
    rank = jnp.sum(jnp.where(hits, within - 1.0 + before[:, :, None], 0.0), axis=0)
    place = (grid * capacity + rank.astype(jnp.int32)).reshape(rows)
    high, lowd = local // 64, local % 64
    filled = jnp.full((groups * capacity,), tile, jnp.int32)
    chosen = place_ids(place, jnp.stack([high, lowd, jnp.ones_like(high)]), groups, capacity)
    sent_ids = jnp.where(chosen[2] > 0.5, (chosen[0] * 64.0 + chosen[1]).astype(jnp.int32), filled)
    return (place, sent_ids.reshape(groups, capacity))


def place_ids(place, digits, groups, capacity):
    slots = groups * capacity
    high, low = place // LANES, place % LANES
    ahead = (high[None, :] == jnp.arange(slots // LANES, dtype=jnp.int32)[:, None])
    behind = (low[None, :] == jnp.arange(LANES, dtype=jnp.int32)[:, None]).astype(jnp.bfloat16)
    out = []
    for d in range(digits.shape[0]):
        left = jnp.where(ahead, digits[d][None, :].astype(jnp.bfloat16), jnp.bfloat16(0))
        out.append(
            lax.dot_general(left, behind, (((1,), (1,)), ((), ())), preferred_element_type=jnp.float32)
        )
    return jnp.stack(out).reshape(digits.shape[0], slots)


def joined(value, axis, combine):
    everything = jax.tree.map(lambda part: lax.all_gather(part, axis), value)
    initial = jax.tree.map(lambda part: part[0], everything)

    def step(k, so_far):
        return combine(so_far, jax.tree.map(lambda part: part[k], everything))

    return lax.fori_loop(1, lax.axis_size(axis), step, initial)


def merge_pair(left, right):
    peak = jnp.maximum(left[0], right[0])
    return (peak, left[1] * jnp.exp(left[0] - peak) + right[1] * jnp.exp(right[0] - peak))


def log_sweeps(projected, firm_rows, log_worker, log_firm):
    worker_tile, firm_tile = projected.shape[0], firm_rows.shape[0]
    height = math.gcd(worker_tile, 512)
    blocks = worker_tile // height

    def surplus(index):
        rows_block = lax.dynamic_slice_in_dim(projected, index * height, height, 0)
        return jnp.dot(rows_block, firm_rows.T, preferred_element_type=jnp.float32)

    def sweep(rounds, carry):
        firm_potential = carry[1]

        def row_stats(index):
            scores = surplus(index) + firm_potential[None, :]
            peak = jnp.max(scores, axis=1)
            return (peak, jnp.sum(jnp.exp(scores - peak[:, None]), axis=1))

        peak, total = lax.map(row_stats, jnp.arange(blocks, dtype=jnp.int32))
        peak, total = joined((peak.reshape(-1), total.reshape(-1)), "af", merge_pair)
        worker_potential = log_worker - (peak + jnp.log(total))

        def col_step(carry, inputs):
            peak, total = carry
            index, shift_block = inputs
            scores = surplus(index) + shift_block[:, None]
            new_peak = jnp.maximum(peak, jnp.max(scores, axis=0))
            total = total * jnp.exp(peak - new_peak) + jnp.sum(
                jnp.exp(scores - new_peak[None, :]), axis=0
            )
            return ((new_peak, total), None)

        start = (
            jnp.full((firm_tile,), -jnp.inf, jnp.float32),
            jnp.zeros((firm_tile,), jnp.float32),
        )
        (peak, total), _ = lax.scan(
            col_step,
            start,
            (jnp.arange(blocks, dtype=jnp.int32), worker_potential.reshape(blocks, height)),
        )
        peak, total = joined((peak, total), "wa", merge_pair)
        return (worker_potential, log_firm - (peak + jnp.log(total)))

    start = (jnp.zeros((worker_tile,), jnp.float32), jnp.zeros((firm_tile,), jnp.float32))
    return lax.fori_loop(0, ITERS, sweep, start)


TINY = 4e-28
LEAST = 1e-25
MOST = 1e30


def sweep_kernel(
    wa_size, af_size, proj_ref, firm_ref, wmass_ref, fmass_ref,
    wsum_ref, fsum_ref, bad_ref,
    e_ref, s_ref, v_ref, u_ref, vb_ref, in_p, in_w, in_h, in_f, in_a, in_b,
    send_sem, recv_sem,
):
    wa, af = lax.axis_index("wa"), lax.axis_index("af")
    wt, ft = proj_ref.shape[0], firm_ref.shape[1]
    wr, fr = wt // LANES, ft // LANES

    barrier = pltpu.get_barrier_semaphore()
    for d in range(1, af_size):
        pl.semaphore_signal(
            barrier, inc=1, device_id=(wa, lax.rem(af + d, af_size)), device_id_type=MESH
        )
    for d in range(1, wa_size):
        pl.semaphore_signal(
            barrier, inc=1, device_id=(lax.rem(wa + d, wa_size), af), device_id_type=MESH
        )

    eye = lax.broadcasted_iota(jnp.int32, (LANES, LANES), 0) == lax.broadcasted_iota(
        jnp.int32, (LANES, LANES), 1
    )

    def lay(column):
        return jnp.sum(jnp.where(eye, column, 0.0), axis=0, keepdims=True)

    def halves(rows):
        row = jnp.concatenate(rows, axis=1)
        top = row.astype(jnp.bfloat16)
        rest = (row - top.astype(jnp.float32)).astype(jnp.bfloat16)
        return jnp.concatenate([top, rest, jnp.zeros((6, row.shape[1]), jnp.bfloat16)], axis=0)

    used = []

    def exchange(inbox, along_af):
        size, me = (af_size, af) if along_af else (wa_size, wa)
        copies = []
        for d in sorted(range(1, size), key=lambda d: abs(2 * d - size)):
            peer = (wa, lax.rem(af + d, size)) if along_af else (lax.rem(wa + d, size), af)
            copies.append(
                pltpu.make_async_remote_copy(
                    src_ref=inbox.at[me],
                    dst_ref=inbox.at[me],
                    send_sem=send_sem.at[len(used)],
                    recv_sem=recv_sem.at[len(used)],
                    device_id=peer,
                    device_id_type=MESH,
                )
            )
            used.append(copies[-1])
            copies[-1].start()
        return copies

    def arrive(copies):
        for copy in copies:
            copy.wait_recv()

    def fill(b, carry):
        spot = pl.ds(pl.multiple_of(b * 256, 256), 256)
        peak = jnp.full((256, LANES), -jnp.inf, jnp.float32)
        for c in range(ft // 512):
            scores = jnp.dot(
                proj_ref[spot, :],
                firm_ref[:, c * 512 : (c + 1) * 512],
                preferred_element_type=jnp.float32,
            )
            s_ref[:, c * 512 : (c + 1) * 512] = scores
            for k in range(4):
                peak = jnp.maximum(peak, scores[:, k * LANES : (k + 1) * LANES])
        peak = jnp.max(peak, axis=1, keepdims=True)
        shift = jnp.broadcast_to(peak, (256, LANES))
        acc = jnp.zeros((256, LANES), jnp.float32)
        for c in range(fr):
            grown = jnp.exp(s_ref[:, c * LANES : (c + 1) * LANES] - shift)
            e_ref[spot, c * LANES : (c + 1) * LANES] = grown.astype(jnp.bfloat16)
            acc = acc + grown
        total = jnp.sum(acc, axis=1, keepdims=True)
        for k in range(2):
            part = slice(k * LANES, (k + 1) * LANES)
            in_p[af, pl.ds(b * 2 + k, 1), :] = lay(total[part])
            in_p[af, pl.ds(wr + b * 2 + k, 1), :] = lay(peak[part])
        return carry

    lax.fori_loop(0, wt // 256, fill, 0)
    pl.semaphore_wait(barrier, af_size + wa_size - 2)

    lead = fr // 4
    group = math.gcd(fr - lead, 4)

    def row_pass(turn, scale):
        vb_ref[...] = v_ref[...].astype(jnp.bfloat16)
        spread = halves([v_ref[c : c + 1, :] for c in range(lead)])

        def block(b, carry):
            spot = pl.ds(pl.multiple_of(b * 256, 256), 256)
            near = lax.dot_general(
                spread,
                e_ref[spot, : lead * LANES],
                (((1,), (1,)), ((), ())),
                preferred_element_type=jnp.float32,
            )
            near = near[0:1] + near[1:2]
            for k in range(2):
                part = pl.ds(pl.multiple_of(b * 256 + k * LANES, LANES), LANES)
                acc = jnp.zeros((LANES, LANES), jnp.float32)
                for c in range(lead, fr, group):
                    terms = [
                        e_ref[part, i * LANES : (i + 1) * LANES] * vb_ref[i : i + 1, :]
                        for i in range(c, c + group)
                    ]
                    while len(terms) > 1:
                        terms = [x + y for x, y in zip(terms[::2], terms[1::2])]
                    acc = acc + terms[0].astype(jnp.float32)
                wsum_ref[pl.ds(b * 2 + k, 1), :] = near[
                    :, k * LANES : (k + 1) * LANES
                ] + lay(jnp.sum(acc, axis=1, keepdims=True))
            return carry

        lax.fori_loop(0, wt // 256, block, 0)
        in_w[turn - 1, af] = wsum_ref[...] * scale

    def col_pass():
        high = math.gcd(wt, 1024)
        lines = high // LANES

        def block(b, acc):
            spot = pl.ds(pl.multiple_of(b * high, high), high)
            lhs = halves([u_ref[pl.ds(b * lines + k, 1), :] for k in range(lines)])
            return acc + jnp.dot(lhs, e_ref[spot, :], preferred_element_type=jnp.float32)

        acc = lax.fori_loop(0, wt // high, block, jnp.zeros((8, ft), jnp.float32))
        total = acc[0:1] + acc[1:2]
        return [total[:, c * LANES : (c + 1) * LANES] for c in range(fr)]

    def least(value):
        return jnp.min(value, axis=0, keepdims=True)

    def most(value):
        return jnp.max(value, axis=0, keepdims=True)

    in_a[wa] = jnp.zeros((16, LANES), jnp.float32)
    in_b[af] = jnp.zeros((16, LANES), jnp.float32)
    for turn in range(ITERS):
        if turn == 0:
            arrive(exchange(in_p, True))
            peaks = [in_p[k, wr:] for k in range(af_size)]
            top = functools.reduce(jnp.maximum, peaks)
            scale = jnp.exp(in_p[af, wr:] - top)
            total = jnp.zeros((wr, LANES), jnp.float32)
            for k in range(af_size):
                total = total + in_p[k, :wr] * jnp.exp(peaks[k] - top)
        else:
            row_pass(turn, scale)
            arrive(exchange(in_w.at[turn - 1], True))
            total = jnp.zeros((wr, LANES), jnp.float32)
            for k in range(af_size):
                total = total + in_w[turn - 1, k]
        u = wmass_ref[...] / total
        u_ref[...] = u * scale
        in_a[wa, turn : turn + 1, :] = least(total)
        in_a[wa, 3 + turn : 4 + turn, :] = most(total)
        in_a[wa, 6 + turn : 7 + turn, :] = most(u)
        in_a[wa, 9 + turn : 10 + turn, :] = least(u)
        final = turn == ITERS - 1
        if final:
            wsum_ref[...] = jnp.log(total) + top
            verdict_a = exchange(in_a, False)
        parts = col_pass()
        if final:
            for c in range(fr):
                in_f[wa, c : c + 1, :] = parts[c]
            arrive(exchange(in_f, False))
        else:
            in_h[turn, wa] = jnp.concatenate(parts, axis=0).astype(jnp.bfloat16)
            arrive(exchange(in_h.at[turn], False))
        total = jnp.zeros((fr, LANES), jnp.float32)
        for k in range(wa_size):
            total = total + (in_f[k] if final else in_h[turn, k].astype(jnp.float32))
        in_b[af, turn : turn + 1, :] = least(total)
        in_b[af, 3 + turn : 4 + turn, :] = most(total)
        if final:
            fsum_ref[...] = jnp.log(total)
        else:
            v = fmass_ref[...] / total
            v_ref[...] = v
            in_b[af, 7 + turn : 8 + turn, :] = most(v)
    in_b[af, 6:7, :] = jnp.ones((1, LANES), jnp.float32)
    verdict_b = exchange(in_b, True)
    arrive(verdict_a)
    low_a = functools.reduce(jnp.minimum, [in_a[k] for k in range(wa_size)])
    high_a = functools.reduce(jnp.maximum, [in_a[k] for k in range(wa_size)])
    low_a = jnp.broadcast_to(jnp.min(low_a, axis=1, keepdims=True), (16, LANES))
    high_a = jnp.broadcast_to(jnp.max(high_a, axis=1, keepdims=True), (16, LANES))
    arrive(verdict_b)
    low_b = functools.reduce(jnp.minimum, [in_b[k] for k in range(af_size)])
    high_b = functools.reduce(jnp.maximum, [in_b[k] for k in range(af_size)])
    low_b = jnp.broadcast_to(jnp.min(low_b, axis=1, keepdims=True), (16, LANES))
    high_b = jnp.broadcast_to(jnp.max(high_b, axis=1, keepdims=True), (16, LANES))
    good = jnp.ones((1, LANES), jnp.float32)
    for turn in range(ITERS):
        row = slice(turn, turn + 1)
        three = slice(3 + turn, 4 + turn)
        six = slice(6 + turn, 7 + turn)
        nine = slice(9 + turn, 10 + turn)
        for ok in (
            low_a[row] > LEAST,
            high_a[three] < MOST,
            high_b[six] * TINY <= low_a[row],
            low_b[row] > LEAST,
            high_b[three] < MOST,
            high_a[six] * TINY <= low_b[row],
            low_a[nine] >= 1e-35,
        ):
            good = jnp.where(ok, good, 0.0)
    bad_ref[...] = jnp.broadcast_to(1.0 - good, (8, LANES))
    for copy in used:
        copy.wait_send()


def fast_sweeps(projected, firm_rows, worker_mass, firm_mass):
    wa_size, af_size = lax.axis_size("wa"), lax.axis_size("af")
    wt, ft = projected.shape[0], firm_rows.shape[0]
    wr, fr = wt // LANES, ft // LANES
    vmem = pl.BlockSpec(memory_space=pltpu.VMEM)
    f32 = jnp.float32
    copies = (ITERS + 1) * (af_size + wa_size - 2)
    return pl.pallas_call(
        functools.partial(sweep_kernel, wa_size, af_size),
        out_shape=(
            jax.ShapeDtypeStruct((wr, LANES), f32),
            jax.ShapeDtypeStruct((fr, LANES), f32),
            jax.ShapeDtypeStruct((8, LANES), f32),
        ),
        in_specs=[vmem] * 4,
        out_specs=(vmem, vmem, vmem),
        scratch_shapes=[
            pltpu.VMEM((wt, ft), jnp.bfloat16),
            pltpu.VMEM((256, ft), f32),
            pltpu.VMEM((fr, LANES), f32),
            pltpu.VMEM((wr, LANES), f32),
            pltpu.VMEM((fr, LANES), jnp.bfloat16),
            pltpu.VMEM((af_size, 2 * wr, LANES), f32),
            pltpu.VMEM((ITERS - 1, af_size, wr, LANES), f32),
            pltpu.VMEM((ITERS - 1, wa_size, fr, LANES), jnp.bfloat16),
            pltpu.VMEM((wa_size, fr, LANES), f32),
            pltpu.VMEM((wa_size, 16, LANES), f32),
            pltpu.VMEM((af_size, 16, LANES), f32),
            pltpu.SemaphoreType.DMA((copies,)),
            pltpu.SemaphoreType.DMA((copies,)),
        ],
        compiler_params=pltpu.CompilerParams(
            collective_id=0, has_side_effects=True, vmem_limit_bytes=VMEM_BYTES
        ),
        name="sweeps",
    )(projected, firm_rows.T, worker_mass.reshape(wr, LANES), firm_mass.reshape(fr, LANES))


def body(worker_ids, worker_attrs, firm_ids, firm_attrs, affinity):
    rows = worker_ids.shape[0]
    wa_count = lax.axis_size("wa")
    af_count = lax.axis_size("af")
    worker_tile = W // wa_count
    firm_tile = F // af_count
    records_all = rows * wa_count * af_count
    cap = 2 * rows // wa_count
    place, sent_ids = pack_records(worker_ids, worker_tile, wa_count, cap)
    worker_part, firm_part, projected, firm_rows, worker_tally, firm_tally = route(
        place, worker_attrs, sent_ids, firm_ids, firm_attrs, affinity, cap
    )
    projected = projected.reshape(worker_tile, LANES)
    firm_rows = firm_rows.reshape(firm_tile, LANES)
    worker_tally = worker_tally[:, : worker_part.shape[0] // LANES].reshape(worker_tile)
    firm_tally = firm_tally[:, : firm_part.shape[0] // LANES].reshape(firm_tile)
    worker_means = lax.all_gather(worker_part, "af", axis=0, tiled=True)
    firm_means = lax.all_gather(firm_part, "wa", axis=0, tiled=True)
    log_worker = jnp.log(worker_tally + 1.0) - jnp.log(jnp.float32(records_all + W))
    log_firm = jnp.log(firm_tally + 1.0) - jnp.log(jnp.float32(records_all + F))
    worker_total, firm_total, bad = fast_sweeps(
        projected,
        firm_rows,
        (worker_tally + 1.0) / jnp.float32(records_all + W),
        (firm_tally + 1.0) / jnp.float32(records_all + F),
    )
    worker_potential, firm_potential = lax.cond(
        bad[0, 0] > 0.5,
        lambda: log_sweeps(projected, firm_rows, log_worker, log_firm),
        lambda: (
            log_worker - worker_total.reshape(-1),
            log_firm - firm_total.reshape(-1),
        ),
    )
    return (
        worker_means,
        firm_means,
        worker_potential,
        firm_potential,
    )


def solution(mesh):
    placed = (P(("wa", "af")), P(("wa", "af"), None), P(("wa", "af")), P(("wa", "af"), None), P())
    return jax.shard_map(
        body,
        mesh=mesh,
        in_specs=placed,
        out_specs=(P("wa", None), P("af", None), P("wa"), P("af")),
        check_vma=False,
    )
```

```python
import functools
import math

import jax
import jax.numpy as jnp
from jax import lax
from jax.experimental import pallas as pl
from jax.experimental.pallas import tpu as pltpu
from jax.sharding import PartitionSpec as P

W = 32768
F = 16384
ITERS = 3
LANES = 128
VMEM_BYTES = 60 * 1024 * 1024
MESH = pl.DeviceIdType.MESH


def upright(row):
    eye = lax.broadcasted_iota(jnp.int32, (LANES, LANES), 0) == lax.broadcasted_iota(
        jnp.int32, (LANES, LANES), 1
    )
    return jnp.sum(jnp.where(eye, row, 0.0), axis=1, keepdims=True)


def route_kernel(
    wa_size, af_size, cap,
    place_ref, wattrs_ref, wids_ref, fids_ref, fattrs_ref, affinity_ref,
    wtop_ref, wrest_ref, frest_ref, proj_ref, frows_ref, wtally_ref, ftally_ref,
    rhs_ref, low_ref, send_ref, inw_ref, idw_ref, inf_ref, idf_ref,
    wpot_ref, fsum_ref, near_w, part_w, far_w, near_f, part_f, far_f,
    send_sem, recv_sem,
):
    wa, af = lax.axis_index("wa"), lax.axis_index("af")
    rows = wattrs_ref.shape[0]
    half = wa_size // 2
    wa_high, af_high = wa_size // 2, af_size // 2
    whole_w, whole_f = proj_ref.shape[1], frows_ref.shape[1]
    wt, ft = whole_w * af_size, whole_f * wa_size
    wa_top, wa_low = wa // 2, lax.rem(wa, 2)
    af_top, af_low = af // 2, lax.rem(af, 2)
    used = [0]

    def copy(src, dst, where):
        slot = used[0]
        used[0] += 1
        return pltpu.make_async_remote_copy(
            src_ref=src,
            dst_ref=dst,
            send_sem=send_sem.at[slot],
            recv_sem=recv_sem.at[slot],
            device_id=where,
            device_id_type=MESH,
        )

    def wa_peer(high, low):
        return (high * 2 + low, af)

    def af_peer(high, low):
        return (wa, high * 2 + low)

    barrier = pltpu.get_barrier_semaphore()
    for d in range(1, wa_size):
        pl.semaphore_signal(
            barrier, inc=1, device_id=(lax.rem(wa + d, wa_size), af), device_id_type=MESH
        )
    for h in range(1, af_high):
        pl.semaphore_signal(
            barrier, inc=1, device_id=af_peer(lax.rem(af_top + h, af_high), af_low),
            device_id_type=MESH,
        )
    pl.semaphore_signal(barrier, inc=1, device_id=af_peer(af_top, 1 - af_low), device_id_type=MESH)

    def split(ids_at, attrs_at, lines, span):
        def fill(c, carry):
            ids = ids_at(c)
            upper = ids >= span
            low_ref[pl.ds(c, 1), :] = jnp.where(upper, ids - span, ids)
            side = upright(jnp.where(upper, 1.0, 0.0))
            spot = pl.ds(pl.multiple_of(c * LANES, LANES), LANES)
            part = attrs_at(spot).astype(jnp.float32)
            rhs_ref[spot, :LANES] = jnp.where(side < 0.5, part, 0.0).astype(jnp.bfloat16)
            rhs_ref[spot, LANES:] = jnp.where(side > 0.5, part, 0.0).astype(jnp.bfloat16)
            return carry

        lax.fori_loop(0, lines, fill, 0, unroll=2)

    def pick(base, block, lines):
        target = lax.broadcasted_iota(jnp.int32, (block, LANES), 0) + base
        step = math.gcd(lines, 8)
        acc = jnp.zeros((block, 2 * LANES), jnp.float32)
        for c in range(0, lines, step):
            hit = jnp.concatenate(
                [
                    jnp.where(low_ref[k : k + 1, :] == target, 1.0, 0.0).astype(jnp.bfloat16)
                    for k in range(c, c + step)
                ],
                axis=1,
            )
            acc = acc + jnp.dot(
                hit,
                rhs_ref[c * LANES : (c + step) * LANES, :],
                preferred_element_type=jnp.float32,
            )
        return acc

    def pool(ids_at, attrs_at, lines, tile, sums_ref, first):
        span = tile // 2
        split(ids_at, attrs_at, lines, span)
        shards, deep, width = sums_ref.shape
        size = deep - 8
        block = math.gcd(math.gcd(span, 1024), size)
        per = size // block

        def step(b, carry):
            acc = pick(b * block, block, lines)
            for side in range(2):
                index = b + side * (span // block)
                spot = pl.ds(pl.multiple_of(lax.rem(index, per) * block, block), block)
                value = acc[:, side * LANES : (side + 1) * LANES]
                if first:
                    sums_ref[index // per, spot, :] = value
                else:
                    sums_ref[index // per, spot, :] += value
            return carry

        lax.fori_loop(0, span // block, step, 0)
        tall = tile // LANES
        total = jnp.zeros((tall, LANES), jnp.float32)
        group = math.gcd(lines, 8)
        for c in range(0, lines, group):
            ahead, behind = [], []
            for k in range(c, c + group):
                ids = ids_at(k)
                high = lax.shift_right_arithmetic(ids, 7)
                rest = ids & (LANES - 1)
                ahead.append(
                    jnp.where(high == lax.broadcasted_iota(jnp.int32, (tall, LANES), 0), 1.0, 0.0)
                )
                behind.append(
                    jnp.where(rest == lax.broadcasted_iota(jnp.int32, (LANES, LANES), 0), 1.0, 0.0)
                )
            total = total + lax.dot_general(
                jnp.concatenate(ahead, axis=1).astype(jnp.bfloat16),
                jnp.concatenate(behind, axis=1).astype(jnp.bfloat16),
                (((1,), (1,)), ((), ())),
                preferred_element_type=jnp.float32,
            )
        counts = size // LANES
        for k in range(shards):
            line = total[k * counts : (k + 1) * counts]
            if first:
                if counts < 8:
                    sums_ref[k, size:, :] = jnp.zeros((8, LANES), jnp.float32)
                sums_ref[k, size : size + counts, :] = line
            else:
                sums_ref[k, size : size + counts, :] += line

    lines = rows // LANES
    cap_lines = cap // LANES
    block = math.gcd(cap, 1024)

    split(lambda c: place_ref[pl.ds(c, 1), :], lambda spot: wattrs_ref[spot, :], lines, half * cap)
    pl.semaphore_wait(barrier, wa_size - 1 + af_high)

    own_high, own_low = [], []
    for h in range(1, af_high):
        where = af_peer(lax.rem(af_top + h, af_high), af_low)
        own_high.append(
            (
                copy(fattrs_ref, inf_ref.at[2 * h], where),
                copy(fids_ref, idf_ref.at[2 * h], where),
            )
        )
    where = af_peer(af_top, 1 - af_low)
    own_low.append(
        (copy(fattrs_ref, inf_ref.at[1], where), copy(fids_ref, idf_ref.at[1], where))
    )
    for pair in own_high + own_low:
        for c in pair:
            c.start()

    sent = {}
    for i in range(half):
        q = lax.rem(wa + i, half)
        one = lax.rem(q - wa + wa_size, wa_size)
        two = lax.rem(one + half, wa_size)

        def fill_block(b, carry):
            acc = pick(q * cap + b * block, block, lines)
            spot = pl.ds(pl.multiple_of(b * block, block), block)
            send_ref[one, spot, :] = acc[:, :LANES].astype(jnp.bfloat16)
            send_ref[two, spot, :] = acc[:, LANES:].astype(jnp.bfloat16)
            return carry

        lax.fori_loop(0, cap // block, fill_block, 0)
        for d in (i + half, i):
            if d:
                to = lax.rem(wa + d, wa_size)
                sent[d] = (
                    copy(send_ref.at[d], inw_ref.at[d - 1], (to, af)),
                    copy(wids_ref.at[to], idw_ref.at[d - 1], (to, af)),
                )
                for c in sent[d]:
                    c.start()

    base = af * ft

    def take_firm(ids_ref, attrs_ref, first):
        pool(
            lambda c: ids_ref[pl.ds(c, 1), :] - base,
            lambda spot: attrs_ref[spot, :],
            lines, ft, fsum_ref, first,
        )

    take_firm(fids_ref, fattrs_ref, True)
    forwards = []
    for h in range(1, af_high):
        for c in own_high[h - 1]:
            c.wait_recv()
        pair = (
            copy(inf_ref.at[2 * h], inf_ref.at[2 * h + 1], af_peer(af_top, 1 - af_low)),
            copy(idf_ref.at[2 * h], idf_ref.at[2 * h + 1], af_peer(af_top, 1 - af_low)),
        )
        for c in pair:
            c.start()
        forwards.append(pair)
    for c in own_low[0]:
        c.wait_recv()
    take_firm(idf_ref.at[1], inf_ref.at[1], False)
    for h in range(1, af_high):
        take_firm(idf_ref.at[2 * h], inf_ref.at[2 * h], False)
    for h in range(1, af_high):
        for c in forwards[h - 1]:
            c.wait_recv()
        take_firm(idf_ref.at[2 * h + 1], inf_ref.at[2 * h + 1], False)

    def scatter_near(sums_ref, near_ref, high, top, low, peer):
        copies = []
        for h in list(range(1, high)) + [0]:
            shard = lax.rem(top + h, high) * 2 + 1 - low
            copies.append(copy(sums_ref.at[shard], near_ref.at[h], peer(top, 1 - low)))
        for c in copies:
            c.start()
        return copies

    def scatter_far(i, copies, out, sums_ref, near_ref, part_ref, far_ref, high, top, low, peer):
        h = (i + 1) % high
        copies[i].wait_recv()
        shard = lax.rem(top + h, high)
        part_ref[h] = sums_ref[shard * 2 + low] + near_ref[h]
        if h:
            out.append(copy(part_ref.at[h], far_ref.at[h - 1], peer(shard, low)))
            out[-1].start()

    def scatter_end(copies, part_ref, far_ref, high):
        for h in range(1, high):
            copies[h - 1].wait_recv()
            part_ref[0] += far_ref[h - 1]

    def spread_far(refs, high, top, low, peer):
        copies = [[] for _ in range(high)]
        mine = top * 2 + low
        for ref in refs:
            for h in range(1, high):
                copies[h].append(copy(ref.at[mine], ref.at[mine], peer(lax.rem(top + h, high), low)))
            copies[0].append(copy(ref.at[mine], ref.at[mine], peer(top, 1 - low)))
        for h in list(range(1, high)) + [0]:
            for c in copies[h]:
                c.start()
        return copies

    def spread_near(copies, refs, high, top, low, peer):
        out = []
        for h in range(1, high):
            for c in copies[h]:
                c.wait_recv()
            origin = lax.rem(top - h + high, high) * 2 + low
            for ref in refs:
                out.append(copy(ref.at[origin], ref.at[origin], peer(top, 1 - low)))
                out[-1].start()
        return out

    at_wa = (wa_high, wa_top, wa_low, wa_peer)
    at_af = (af_high, af_top, af_low, af_peer)

    near_firm = scatter_near(fsum_ref, near_f, *at_wa)

    def take_worker(d, first=False):
        if d:
            for c in sent[d]:
                c.wait_recv()
            ids, attrs = idw_ref.at[d - 1], inw_ref.at[d - 1]
        else:
            ids, attrs = wids_ref.at[wa], send_ref.at[0]
        pool(
            lambda c: ids[pl.ds(c, 1), :],
            lambda spot: attrs[spot, :],
            cap_lines, wt, wpot_ref, first,
        )

    order = [0]
    for i in range(half):
        order += [d for d in (i + half, i) if d]
    far_firm, far_worker, step = [], [], 0
    for n, d in enumerate(order):
        take_worker(d, n == 0)
        if n >= 2 and n % 2 == 0 and step < wa_high - 1:
            scatter_far(step, near_firm, far_firm, fsum_ref, near_f, part_f, far_f, *at_wa)
            step += 1

    near_worker = scatter_near(wpot_ref, near_w, *at_af)
    for i in range(step, wa_high):
        scatter_far(i, near_firm, far_firm, fsum_ref, near_f, part_f, far_f, *at_wa)
    for i in range(af_high):
        scatter_far(i, near_worker, far_worker, wpot_ref, near_w, part_w, far_w, *at_af)

    def finish_means(part_ref, size, emit):
        def step(r, carry):
            tally = upright(part_ref[0, pl.ds(size + r, 1), :])
            spot = pl.ds(pl.multiple_of(r * LANES, LANES), LANES)
            means = part_ref[0, spot, :] / jnp.maximum(tally, 1.0)
            top = means.astype(jnp.bfloat16)
            emit(spot, top, (means - top.astype(jnp.float32)).astype(jnp.bfloat16))
            return carry

        lax.fori_loop(0, size // LANES, step, 0)

    def emit_worker(spot, means, rest):
        wtop_ref[spot, :] = means
        wrest_ref[spot, :] = rest
        proj_ref[af, spot, :] = jnp.dot(
            means, affinity_ref[...], preferred_element_type=jnp.float32
        ).astype(jnp.bfloat16)

    def emit_firm(spot, means, rest):
        frest_ref[spot, :] = rest
        frows_ref[wa, spot, :] = means

    scatter_end(far_worker, part_w, far_w, af_high)
    finish_means(part_w, whole_w, emit_worker)
    wtally_ref[af] = part_w[0, whole_w:, :]
    worker_far = spread_far((proj_ref, wtally_ref), *at_af)
    scatter_end(far_firm, part_f, far_f, wa_high)
    finish_means(part_f, whole_f, emit_firm)
    ftally_ref[wa] = part_f[0, whole_f:, :]
    firm_far = spread_far((frows_ref, ftally_ref), *at_wa)
    worker_near = spread_near(worker_far, (proj_ref, wtally_ref), *at_af)
    firm_near = spread_near(firm_far, (frows_ref, ftally_ref), *at_wa)
    for c in worker_far[0] + firm_far[0] + worker_near + firm_near:
        c.wait_recv()
    done = [c for pair in own_high + own_low + forwards + list(sent.values()) for c in pair]
    done += near_firm + near_worker + far_firm + far_worker + worker_near + firm_near
    done += [c for group in worker_far + firm_far for c in group]
    for c in done:
        c.wait_send()


def route(place, worker_attrs, sent_ids, firm_ids, firm_attrs, affinity, cap):
    wa_size, af_size = lax.axis_size("wa"), lax.axis_size("af")
    rows = worker_attrs.shape[0]
    wt, ft = W // wa_size, F // af_size
    sw, sf = wt // af_size, ft // wa_size
    lines = rows // LANES
    wa_high, af_high = wa_size // 2, af_size // 2
    vmem = pl.BlockSpec(memory_space=pltpu.VMEM)
    f32, bf16, i32 = jnp.float32, jnp.bfloat16, jnp.int32
    copies = 4 * af_high + 2 * (wa_size - 1) + 4 * (wa_high + af_high)
    copies += 4 * (wa_high + af_high)
    return pl.pallas_call(
        functools.partial(route_kernel, wa_size, af_size, cap),
        out_shape=(
            jax.ShapeDtypeStruct((sw, LANES), bf16),
            jax.ShapeDtypeStruct((sw, LANES), bf16),
            jax.ShapeDtypeStruct((sf, LANES), bf16),
            jax.ShapeDtypeStruct((af_size, sw, LANES), bf16),
            jax.ShapeDtypeStruct((wa_size, sf, LANES), bf16),
            jax.ShapeDtypeStruct((af_size, 8, LANES), f32),
            jax.ShapeDtypeStruct((wa_size, 8, LANES), f32),
        ),
        in_specs=[vmem] * 6,
        out_specs=(vmem,) * 7,
        scratch_shapes=[
            pltpu.VMEM((rows, 2 * LANES), bf16),
            pltpu.VMEM((lines, LANES), i32),
            pltpu.VMEM((wa_size, cap, LANES), bf16),
            pltpu.VMEM((wa_size - 1, cap, LANES), bf16),
            pltpu.VMEM((wa_size - 1, cap // LANES, LANES), i32),
            pltpu.VMEM((af_size, rows, LANES), bf16),
            pltpu.VMEM((af_size, lines, LANES), i32),
            pltpu.VMEM((af_size, sw + 8, LANES), f32),
            pltpu.VMEM((wa_size, sf + 8, LANES), f32),
            pltpu.VMEM((af_high, sw + 8, LANES), f32),
            pltpu.VMEM((af_high, sw + 8, LANES), f32),
            pltpu.VMEM((max(af_high - 1, 1), sw + 8, LANES), f32),
            pltpu.VMEM((wa_high, sf + 8, LANES), f32),
            pltpu.VMEM((wa_high, sf + 8, LANES), f32),
            pltpu.VMEM((max(wa_high - 1, 1), sf + 8, LANES), f32),
            pltpu.SemaphoreType.DMA((copies,)),
            pltpu.SemaphoreType.DMA((copies,)),
        ],
        compiler_params=pltpu.CompilerParams(
            collective_id=1, has_side_effects=True, vmem_limit_bytes=VMEM_BYTES
        ),
        name="route",
    )(
        place.reshape(lines, LANES),
        worker_attrs,
        sent_ids.reshape(wa_size, cap // LANES, LANES),
        firm_ids.reshape(lines, LANES),
        firm_attrs,
        affinity,
    )


def pack_records(type_ids, tile, groups, capacity):
    rows = type_ids.shape[0]
    owner = type_ids // tile
    local = type_ids - owner * tile
    grid = owner.reshape(rows // LANES, LANES)
    hits = (grid[None] == jnp.arange(groups, dtype=jnp.int32)[:, None, None])
    ramp = jnp.arange(LANES, dtype=jnp.int32)
    upper = (ramp[:, None] <= ramp[None, :]).astype(jnp.bfloat16)
    within = jnp.dot(hits.astype(jnp.bfloat16), upper, preferred_element_type=jnp.float32)
    lines = within[:, :, -1]
    line = jnp.arange(rows // LANES, dtype=jnp.int32)
    before = jnp.sum(
        jnp.where(line[None, :, None] < line[None, None, :], lines[:, :, None], 0.0), axis=1
    )
    rank = jnp.sum(jnp.where(hits, within - 1.0 + before[:, :, None], 0.0), axis=0)
    place = (grid * capacity + rank.astype(jnp.int32)).reshape(rows)
    high, lowd = local // 64, local % 64
    filled = jnp.full((groups * capacity,), tile, jnp.int32)
    chosen = place_ids(place, jnp.stack([high, lowd, jnp.ones_like(high)]), groups, capacity)
    sent_ids = jnp.where(chosen[2] > 0.5, (chosen[0] * 64.0 + chosen[1]).astype(jnp.int32), filled)
    return (place, sent_ids.reshape(groups, capacity))


def place_ids(place, digits, groups, capacity):
    slots = groups * capacity
    high, low = place // LANES, place % LANES
    ahead = (high[None, :] == jnp.arange(slots // LANES, dtype=jnp.int32)[:, None])
    behind = (low[None, :] == jnp.arange(LANES, dtype=jnp.int32)[:, None]).astype(jnp.bfloat16)
    out = []
    for d in range(digits.shape[0]):
        left = jnp.where(ahead, digits[d][None, :].astype(jnp.bfloat16), jnp.bfloat16(0))
        out.append(
            lax.dot_general(left, behind, (((1,), (1,)), ((), ())), preferred_element_type=jnp.float32)
        )
    return jnp.stack(out).reshape(digits.shape[0], slots)


def joined(value, axis, combine):
    everything = jax.tree.map(lambda part: lax.all_gather(part, axis), value)
    initial = jax.tree.map(lambda part: part[0], everything)

    def step(k, so_far):
        return combine(so_far, jax.tree.map(lambda part: part[k], everything))

    return lax.fori_loop(1, lax.axis_size(axis), step, initial)


def merge_pair(left, right):
    peak = jnp.maximum(left[0], right[0])
    return (peak, left[1] * jnp.exp(left[0] - peak) + right[1] * jnp.exp(right[0] - peak))


def log_sweeps(projected, firm_rows, log_worker, log_firm):
    worker_tile, firm_tile = projected.shape[0], firm_rows.shape[0]
    height = math.gcd(worker_tile, 512)
    blocks = worker_tile // height

    def surplus(index):
        rows_block = lax.dynamic_slice_in_dim(projected, index * height, height, 0)
        return jnp.dot(rows_block, firm_rows.T, preferred_element_type=jnp.float32)

    def sweep(rounds, carry):
        firm_potential = carry[1]

        def row_stats(index):
            scores = surplus(index) + firm_potential[None, :]
            peak = jnp.max(scores, axis=1)
            return (peak, jnp.sum(jnp.exp(scores - peak[:, None]), axis=1))

        peak, total = lax.map(row_stats, jnp.arange(blocks, dtype=jnp.int32))
        peak, total = joined((peak.reshape(-1), total.reshape(-1)), "af", merge_pair)
        worker_potential = log_worker - (peak + jnp.log(total))

        def col_step(carry, inputs):
            peak, total = carry
            index, shift_block = inputs
            scores = surplus(index) + shift_block[:, None]
            new_peak = jnp.maximum(peak, jnp.max(scores, axis=0))
            total = total * jnp.exp(peak - new_peak) + jnp.sum(
                jnp.exp(scores - new_peak[None, :]), axis=0
            )
            return ((new_peak, total), None)

        start = (
            jnp.full((firm_tile,), -jnp.inf, jnp.float32),
            jnp.zeros((firm_tile,), jnp.float32),
        )
        (peak, total), _ = lax.scan(
            col_step,
            start,
            (jnp.arange(blocks, dtype=jnp.int32), worker_potential.reshape(blocks, height)),
        )
        peak, total = joined((peak, total), "wa", merge_pair)
        return (worker_potential, log_firm - (peak + jnp.log(total)))

    start = (jnp.zeros((worker_tile,), jnp.float32), jnp.zeros((firm_tile,), jnp.float32))
    return lax.fori_loop(0, ITERS, sweep, start)


TINY = 4e-28
LEAST = 1e-25
MOST = 1e30


def sweep_kernel(
    wa_size, af_size, records, proj_ref, rows_ref, wtally_ref, ftally_ref, wtop_ref, wrest_ref, frest_ref,
    wpot_ref, fpot_ref, bad_ref, wtops_ref, wrests_ref, frests_ref,
    e_ref, s_ref, firm_ref, v_ref, u_ref, vb_ref, col_ref, wplus_ref, fplus_ref,
    in_p, in_w, in_h, in_f, in_a, in_b, send_sem, recv_sem,
):
    wa, af = lax.axis_index("wa"), lax.axis_index("af")
    wt, ft = proj_ref.shape[0], rows_ref.shape[0]
    wr, fr = wt // LANES, ft // LANES
    wa_high, af_high = wa_size // 2, af_size // 2
    wa_top, wa_low = wa // 2, lax.rem(wa, 2)
    af_top, af_low = af // 2, lax.rem(af, 2)
    worker_all, firm_all = float(records + W), float(records + F)

    barrier = pltpu.get_barrier_semaphore()
    for d in range(1, af_size):
        pl.semaphore_signal(
            barrier, inc=1, device_id=(wa, lax.rem(af + d, af_size)), device_id_type=MESH
        )
    for d in range(1, wa_size):
        pl.semaphore_signal(
            barrier, inc=1, device_id=(lax.rem(wa + d, wa_size), af), device_id_type=MESH
        )

    eye = lax.broadcasted_iota(jnp.int32, (LANES, LANES), 0) == lax.broadcasted_iota(
        jnp.int32, (LANES, LANES), 1
    )

    def lay(column):
        return jnp.sum(jnp.where(eye, column, 0.0), axis=0, keepdims=True)

    def halves(rows):
        row = jnp.concatenate(rows, axis=1)
        top = row.astype(jnp.bfloat16)
        rest = (row - top.astype(jnp.float32)).astype(jnp.bfloat16)
        return jnp.concatenate([top, rest, jnp.zeros((6, row.shape[1]), jnp.bfloat16)], axis=0)

    used = []

    def push(ref, index, peer):
        used.append(
            pltpu.make_async_remote_copy(
                src_ref=ref.at[index],
                dst_ref=ref.at[index],
                send_sem=send_sem.at[len(used)],
                recv_sem=recv_sem.at[len(used)],
                device_id=peer,
                device_id_type=MESH,
            )
        )
        used[-1].start()
        return used[-1]

    def exchange(inbox, along_af):
        size, me = (af_size, af) if along_af else (wa_size, wa)
        copies = []
        for d in sorted(range(1, size), key=lambda d: abs(2 * d - size)):
            peer = (wa, lax.rem(af + d, size)) if along_af else (lax.rem(wa + d, size), af)
            copies.append(push(inbox, me, peer))
        return copies

    def arrive(copies):
        for copy in copies:
            copy.wait_recv()

    hr, hf = wr // 2, fr // 2

    def fill(p, start, stop):
        def block(b, carry):
            spot = pl.ds(pl.multiple_of(p * hr * LANES + b * 256, 256), 256)
            peak = jnp.full((256, LANES), -jnp.inf, jnp.float32)
            for c in range(ft // 512):
                scores = jnp.dot(
                    proj_ref[spot, :],
                    firm_ref[:, c * 512 : (c + 1) * 512],
                    preferred_element_type=jnp.float32,
                )
                s_ref[:, c * 512 : (c + 1) * 512] = scores
                for k in range(4):
                    peak = jnp.maximum(peak, scores[:, k * LANES : (k + 1) * LANES])
            peak = jnp.max(peak, axis=1, keepdims=True)
            shift = jnp.broadcast_to(peak, (256, LANES))
            acc = jnp.zeros((256, LANES), jnp.float32)
            for c in range(fr):
                grown = jnp.exp(s_ref[:, c * LANES : (c + 1) * LANES] - shift)
                e_ref[spot, c * LANES : (c + 1) * LANES] = grown.astype(jnp.bfloat16)
                acc = acc + grown
            total = jnp.sum(acc, axis=1, keepdims=True)
            for k in range(2):
                part = slice(k * LANES, (k + 1) * LANES)
                in_p[p, af, pl.ds(b * 2 + k, 1), :] = lay(total[part])
                in_p[p, af, pl.ds(hr + b * 2 + k, 1), :] = lay(peak[part])
            return carry

        lax.fori_loop(start, stop, block, 0)

    lead = hf // 4
    group = math.gcd(hf - lead, 4)

    def row_pass(p, g):
        first, last = g * hf, (g + 1) * hf
        spread = halves([v_ref[c : c + 1, :] for c in range(first, first + lead)])

        def block(b, carry):
            spot = pl.ds(pl.multiple_of(p * hr * LANES + b * 256, 256), 256)
            near = lax.dot_general(
                spread,
                e_ref[spot, first * LANES : (first + lead) * LANES],
                (((1,), (1,)), ((), ())),
                preferred_element_type=jnp.float32,
            )
            near = near[0:1] + near[1:2]
            for k in range(2):
                part = pl.ds(
                    pl.multiple_of((p * hr + k) * LANES + b * 256, LANES), LANES
                )
                acc = jnp.zeros((LANES, LANES), jnp.float32)
                for c in range(first + lead, last, group):
                    terms = [
                        e_ref[part, i * LANES : (i + 1) * LANES] * vb_ref[i : i + 1, :]
                        for i in range(c, c + group)
                    ]
                    while len(terms) > 1:
                        terms = [x + y for x, y in zip(terms[::2], terms[1::2])]
                    acc = acc + terms[0].astype(jnp.float32)
                row = near[:, k * LANES : (k + 1) * LANES] + lay(
                    jnp.sum(acc, axis=1, keepdims=True)
                )
                line = pl.ds(p * hr + b * 2 + k, 1)
                if g:
                    row = row + wpot_ref[line, :]
                wpot_ref[line, :] = row
            return carry

        lax.fori_loop(0, hr // 2, block, 0)

    def col_pass(p, g):
        deep = hr * LANES
        high = math.gcd(deep, 1024)
        lines = high // LANES
        span = slice(g * hf * LANES, (g + 1) * hf * LANES)

        def block(b, acc):
            spot = pl.ds(pl.multiple_of(p * deep + b * high, high), high)
            lhs = halves([u_ref[pl.ds(p * hr + b * lines + k, 1), :] for k in range(lines)])
            return acc + jnp.dot(lhs, e_ref[spot, span], preferred_element_type=jnp.float32)

        start = jnp.zeros((8, hf * LANES), jnp.float32) if p == 0 else col_ref[g]
        acc = lax.fori_loop(0, deep // high, block, start)
        if p == 0:
            col_ref[g] = acc
            return None
        total = acc[0:1] + acc[1:2]
        return [total[:, c * LANES : (c + 1) * LANES] for c in range(hf)]

    def least(value):
        return jnp.min(value, axis=0, keepdims=True)

    def most(value):
        return jnp.max(value, axis=0, keepdims=True)

    in_a[wa] = jnp.zeros((16, LANES), jnp.float32)
    in_b[af] = jnp.zeros((16, LANES), jnp.float32)
    for ref, tally_ref, per in (
        (wplus_ref, wtally_ref, wr // af_size),
        (fplus_ref, ftally_ref, fr // wa_size),
    ):
        for k in range(tally_ref.shape[0]):
            ref[k * per : (k + 1) * per, :] = tally_ref[k, :per, :] + 1.0
    for c in range(fr):
        spot = slice(c * LANES, (c + 1) * LANES)
        firm_ref[:, spot] = rows_ref[spot, :].astype(jnp.float32).T.astype(jnp.bfloat16)
    wtops_ref[af] = wtop_ref[...]
    wrests_ref[af] = wrest_ref[...]
    frests_ref[wa] = frest_ref[...]
    steps = hr // 2
    fill(0, 0, steps // 4)
    pl.semaphore_wait(barrier, af_size + wa_size - 2)
    worker_far = [
        push(ref, af, (wa, lax.rem(af_top + h, af_high) * 2 + af_low))
        for h in range(1, af_high)
        for ref in (wtops_ref, wrests_ref)
    ]
    firm_far = [
        push(frests_ref, wa, (lax.rem(wa_top + h, wa_high) * 2 + wa_low, af))
        for h in range(1, wa_high)
    ]
    beside_w, beside_f = (wa, af_top * 2 + 1 - af_low), (wa_top * 2 + 1 - wa_low, af)
    near = [push(frests_ref, wa, beside_f)]
    near += [push(ref, af, beside_w) for ref in (wtops_ref, wrests_ref)]
    fill(0, steps // 4, steps)
    moving = [exchange(in_p.at[0], True)]
    fill(1, 0, steps // 2)
    for h in range(1, wa_high):
        firm_far[h - 1].wait_recv()
        origin = lax.rem(wa_top - h + wa_high, wa_high) * 2 + wa_low
        near.append(push(frests_ref, origin, beside_f))
    for h in range(1, af_high):
        origin = lax.rem(af_top - h + af_high, af_high) * 2 + af_low
        for i, ref in enumerate((wtops_ref, wrests_ref)):
            worker_far[2 * (h - 1) + i].wait_recv()
            near.append(push(ref, origin, beside_w))
    fill(1, steps // 2, steps)
    moving.append(exchange(in_p.at[1], True))
    scale, top = [None, None], [None, None]
    for turn in range(ITERS):
        final = turn == ITERS - 1
        stats = []
        for p in range(2):
            arrive(moving[p])
            total = jnp.zeros((hr, LANES), jnp.float32)
            if turn == 0:
                peaks = [in_p[p, k, hr:] for k in range(af_size)]
                top[p] = functools.reduce(jnp.maximum, peaks)
                scale[p] = jnp.exp(in_p[p, af, hr:] - top[p])
                for k in range(af_size):
                    total = total + in_p[p, k, :hr] * jnp.exp(peaks[k] - top[p])
            else:
                for k in range(af_size):
                    total = total + in_w[(turn - 1) * 2 + p, k]
            here = slice(p * hr, (p + 1) * hr)
            u = (wplus_ref[here, :] / worker_all) / total
            u_ref[here, :] = u * scale[p]
            stats.append((least(total), most(total), most(u), least(u)))
            if final:
                log_a = jnp.log(wplus_ref[here, :]) - math.log(worker_all)
                wpot_ref[here, :] = log_a - (top[p] + jnp.log(total))
            if p == 0:
                col_pass(0, 0)
                col_pass(0, 1)
        one, two = stats
        in_a[wa, turn : turn + 1, :] = jnp.minimum(one[0], two[0])
        in_a[wa, 3 + turn : 4 + turn, :] = jnp.maximum(one[1], two[1])
        in_a[wa, 6 + turn : 7 + turn, :] = jnp.maximum(one[2], two[2])
        in_a[wa, 9 + turn : 10 + turn, :] = jnp.minimum(one[3], two[3])
        moving = []
        for g in range(2):
            parts = col_pass(1, g)
            if final:
                for c in range(hf):
                    in_f[g, wa, c : c + 1, :] = parts[c]
                moving.append(exchange(in_f.at[g], False))
            else:
                in_h[turn * 2 + g, wa] = jnp.concatenate(parts, axis=0).astype(in_h.dtype)
                moving.append(exchange(in_h.at[turn * 2 + g], False))
        if final:
            verdict_a = exchange(in_a, False)
        stats = []
        for g in range(2):
            arrive(moving[g])
            total = jnp.zeros((hf, LANES), jnp.float32)
            for k in range(wa_size):
                total = total + (
                    in_f[g, k] if final else in_h[turn * 2 + g, k].astype(jnp.float32)
                )
            here = slice(g * hf, (g + 1) * hf)
            if final:
                log_b = jnp.log(fplus_ref[here, :]) - math.log(firm_all)
                fpot_ref[here, :] = log_b - jnp.log(total)
                stats.append((least(total), most(total)))
            else:
                v = (fplus_ref[here, :] / firm_all) / total
                v_ref[here, :] = v
                vb_ref[here, :] = v.astype(vb_ref.dtype)
                stats.append((least(total), most(total), most(v)))
                if g == 0:
                    row_pass(0, 0)
                    row_pass(1, 0)
                else:
                    moving = []
                    for p in range(2):
                        row_pass(p, 1)
                        spot = slice(p * hr, (p + 1) * hr)
                        in_w[turn * 2 + p, af] = wpot_ref[spot, :] * scale[p]
                        moving.append(exchange(in_w.at[turn * 2 + p], True))
        one, two = stats
        in_b[af, turn : turn + 1, :] = jnp.minimum(one[0], two[0])
        in_b[af, 3 + turn : 4 + turn, :] = jnp.maximum(one[1], two[1])
        if not final:
            in_b[af, 7 + turn : 8 + turn, :] = jnp.maximum(one[2], two[2])
    in_b[af, 6:7, :] = jnp.ones((1, LANES), jnp.float32)
    verdict_b = exchange(in_b, True)
    arrive(verdict_a)
    low_a = functools.reduce(jnp.minimum, [in_a[k] for k in range(wa_size)])
    high_a = functools.reduce(jnp.maximum, [in_a[k] for k in range(wa_size)])
    low_a = jnp.broadcast_to(jnp.min(low_a, axis=1, keepdims=True), (16, LANES))
    high_a = jnp.broadcast_to(jnp.max(high_a, axis=1, keepdims=True), (16, LANES))
    arrive(verdict_b)
    low_b = functools.reduce(jnp.minimum, [in_b[k] for k in range(af_size)])
    high_b = functools.reduce(jnp.maximum, [in_b[k] for k in range(af_size)])
    low_b = jnp.broadcast_to(jnp.min(low_b, axis=1, keepdims=True), (16, LANES))
    high_b = jnp.broadcast_to(jnp.max(high_b, axis=1, keepdims=True), (16, LANES))
    good = jnp.ones((1, LANES), jnp.float32)
    for turn in range(ITERS):
        row = slice(turn, turn + 1)
        three = slice(3 + turn, 4 + turn)
        six = slice(6 + turn, 7 + turn)
        nine = slice(9 + turn, 10 + turn)
        for ok in (
            low_a[row] > LEAST,
            high_a[three] < MOST,
            high_b[six] * TINY <= low_a[row],
            low_b[row] > LEAST,
            high_b[three] < MOST,
            high_a[six] * TINY <= low_b[row],
            low_a[nine] >= 1e-35,
        ):
            good = jnp.where(ok, good, 0.0)
    bad_ref[0, 0] = 1.0 - jnp.min(good)
    arrive(near)
    for copy in used:
        copy.wait_send()


def fast_sweeps(projected, firm_rows, worker_tally, firm_tally, worker_top, worker_rest, firm_rest, records):
    wa_size, af_size = lax.axis_size("wa"), lax.axis_size("af")
    wt, ft = projected.shape[0], firm_rows.shape[0]
    wr, fr = wt // LANES, ft // LANES
    vmem = pl.BlockSpec(memory_space=pltpu.VMEM)
    f32 = jnp.float32
    copies = (2 * ITERS + 2) * (af_size + wa_size - 2) + af_size
    hr, hf = wr // 2, fr // 2
    kind = jnp.bfloat16 if hf % 16 == 0 else f32
    return pl.pallas_call(
        functools.partial(sweep_kernel, wa_size, af_size, records),
        out_shape=(
            jax.ShapeDtypeStruct((wr, LANES), f32),
            jax.ShapeDtypeStruct((fr, LANES), f32),
            jax.ShapeDtypeStruct((1, 1), f32),
            jax.ShapeDtypeStruct((af_size,) + worker_top.shape, jnp.bfloat16),
            jax.ShapeDtypeStruct((af_size,) + worker_top.shape, jnp.bfloat16),
            jax.ShapeDtypeStruct((wa_size,) + firm_rest.shape, jnp.bfloat16),
        ),
        in_specs=[vmem] * 7,
        out_specs=(vmem, vmem, pl.BlockSpec(memory_space=pltpu.SMEM), vmem, vmem, vmem),
        scratch_shapes=[
            pltpu.VMEM((wt, ft), jnp.bfloat16),
            pltpu.VMEM((256, ft), f32),
            pltpu.VMEM((LANES, ft), jnp.bfloat16),
            pltpu.VMEM((fr, LANES), f32),
            pltpu.VMEM((wr, LANES), f32),
            pltpu.VMEM((fr, LANES), jnp.bfloat16 if fr % 32 == 0 else f32),
            pltpu.VMEM((2, 8, hf * LANES), f32),
            pltpu.VMEM((wr, LANES), f32),
            pltpu.VMEM((fr, LANES), f32),
            pltpu.VMEM((2, af_size, 2 * hr, LANES), f32),
            pltpu.VMEM(((ITERS - 1) * 2, af_size, hr, LANES), f32),
            pltpu.VMEM(((ITERS - 1) * 2, wa_size, hf, LANES), kind),
            pltpu.VMEM((2, wa_size, hf, LANES), f32),
            pltpu.VMEM((wa_size, 16, LANES), f32),
            pltpu.VMEM((af_size, 16, LANES), f32),
            pltpu.SemaphoreType.DMA((copies,)),
            pltpu.SemaphoreType.DMA((copies,)),
        ],
        compiler_params=pltpu.CompilerParams(
            collective_id=0, has_side_effects=True, vmem_limit_bytes=VMEM_BYTES
        ),
        name="sweeps",
    )(projected, firm_rows, worker_tally, firm_tally, worker_top, worker_rest, firm_rest)


def body(worker_ids, worker_attrs, firm_ids, firm_attrs, affinity):
    rows = worker_ids.shape[0]
    wa_count = lax.axis_size("wa")
    af_count = lax.axis_size("af")
    worker_tile = W // wa_count
    firm_tile = F // af_count
    records_all = rows * wa_count * af_count
    cap = 2 * rows // wa_count
    place, sent_ids = pack_records(worker_ids, worker_tile, wa_count, cap)
    worker_top, worker_rest, firm_rest, projected, firm_rows, worker_tally, firm_tally = route(
        place, worker_attrs, sent_ids, firm_ids, firm_attrs, affinity, cap
    )
    projected = projected.reshape(worker_tile, LANES)
    firm_rows = firm_rows.reshape(firm_tile, LANES)
    worker_potential, firm_potential, bad, tops, rests, firm_rests = fast_sweeps(
        projected, firm_rows, worker_tally, firm_tally,
        worker_top, worker_rest, firm_rest, records_all,
    )

    def whole(top, rest):
        return top.reshape(-1, LANES).astype(jnp.float32) + rest.reshape(-1, LANES).astype(
            jnp.float32
        )

    worker_means = whole(tops, rests)
    firm_means = whole(firm_rows, firm_rests)

    def careful():
        worker_each = worker_tally[:, : worker_top.shape[0] // LANES].reshape(worker_tile)
        firm_each = firm_tally[:, : firm_rest.shape[0] // LANES].reshape(firm_tile)
        log_worker = jnp.log(worker_each + 1.0) - jnp.log(jnp.float32(records_all + W))
        log_firm = jnp.log(firm_each + 1.0) - jnp.log(jnp.float32(records_all + F))
        return log_sweeps(projected, firm_rows, log_worker, log_firm)

    worker_potential, firm_potential = lax.cond(
        bad[0, 0] > 0.5,
        careful,
        lambda: (worker_potential.reshape(-1), firm_potential.reshape(-1)),
    )
    return (
        worker_means,
        firm_means,
        worker_potential,
        firm_potential,
    )


def solution(mesh):
    placed = (P(("wa", "af")), P(("wa", "af"), None), P(("wa", "af")), P(("wa", "af"), None), P())
    return jax.shard_map(
        body,
        mesh=mesh,
        in_specs=placed,
        out_specs=(P("wa", None), P("af", None), P("wa"), P("af")),
        check_vma=False,
    )
```

```python
import functools
import math

import jax
import jax.numpy as jnp
from jax import lax
from jax.experimental import pallas as pl
from jax.experimental.pallas import tpu as pltpu
from jax.sharding import PartitionSpec as P

W = 32768
F = 16384
ITERS = 3
LANES = 128
VMEM_BYTES = 60 * 1024 * 1024
MESH = pl.DeviceIdType.MESH


def upright(row):
    eye = lax.broadcasted_iota(jnp.int32, (LANES, LANES), 0) == lax.broadcasted_iota(
        jnp.int32, (LANES, LANES), 1
    )
    return jnp.sum(jnp.where(eye, row, 0.0), axis=1, keepdims=True)


def route_kernel(
    wa_size, af_size, cap,
    place_ref, wattrs_ref, wids_ref, fids_ref, fattrs_ref, affinity_ref,
    wtop_ref, wrest_ref, frest_ref, proj_ref, frows_ref, wtally_ref, ftally_ref,
    rhs_ref, low_ref, send_ref, inw_ref, idw_ref, inf_ref, idf_ref,
    wsum_ref, fsum_ref, near_w, part_w, far_w, near_f, part_f, far_f,
    send_sem, recv_sem,
):
    wa, af = lax.axis_index("wa"), lax.axis_index("af")
    rows = wattrs_ref.shape[0]
    half = wa_size // 2
    wa_high, af_high = wa_size // 2, af_size // 2
    whole_w, whole_f = proj_ref.shape[1], frows_ref.shape[1]
    wt, ft = whole_w * af_size, whole_f * wa_size
    wa_top, wa_low = wa // 2, lax.rem(wa, 2)
    af_top, af_low = af // 2, lax.rem(af, 2)
    used = [0]

    def copy(src, dst, where):
        slot = used[0]
        used[0] += 1
        return pltpu.make_async_remote_copy(
            src_ref=src,
            dst_ref=dst,
            send_sem=send_sem.at[slot],
            recv_sem=recv_sem.at[slot],
            device_id=where,
            device_id_type=MESH,
        )

    def wa_peer(high, low):
        return (high * 2 + low, af)

    def af_peer(high, low):
        return (wa, high * 2 + low)

    barrier = pltpu.get_barrier_semaphore()
    for d in range(1, wa_size):
        pl.semaphore_signal(
            barrier, inc=1, device_id=(lax.rem(wa + d, wa_size), af), device_id_type=MESH
        )
    for h in range(1, af_high):
        pl.semaphore_signal(
            barrier, inc=1, device_id=af_peer(lax.rem(af_top + h, af_high), af_low),
            device_id_type=MESH,
        )
    pl.semaphore_signal(barrier, inc=1, device_id=af_peer(af_top, 1 - af_low), device_id_type=MESH)

    def split(ids_at, attrs_at, lines, span):
        def fill(c, carry):
            ids = ids_at(c)
            upper = ids >= span
            low_ref[pl.ds(c, 1), :] = jnp.where(upper, ids - span, ids)
            side = upright(jnp.where(upper, 1.0, 0.0))
            spot = pl.ds(pl.multiple_of(c * LANES, LANES), LANES)
            part = attrs_at(spot).astype(jnp.float32)
            rhs_ref[spot, :LANES] = jnp.where(side < 0.5, part, 0.0).astype(jnp.bfloat16)
            rhs_ref[spot, LANES:] = jnp.where(side > 0.5, part, 0.0).astype(jnp.bfloat16)
            return carry

        lax.fori_loop(0, lines, fill, 0, unroll=2)

    def pick(base, block, lines):
        target = lax.broadcasted_iota(jnp.int32, (block, LANES), 0) + base
        step = math.gcd(lines, 8)
        acc = jnp.zeros((block, 2 * LANES), jnp.float32)
        for c in range(0, lines, step):
            hit = jnp.concatenate(
                [
                    jnp.where(low_ref[k : k + 1, :] == target, 1.0, 0.0).astype(jnp.bfloat16)
                    for k in range(c, c + step)
                ],
                axis=1,
            )
            acc = acc + jnp.dot(
                hit,
                rhs_ref[c * LANES : (c + step) * LANES, :],
                preferred_element_type=jnp.float32,
            )
        return acc

    def pool(ids_at, attrs_at, lines, tile, sums_ref, first, turns=None):
        span = tile // 2
        split(ids_at, attrs_at, lines, span)
        shards, deep, width = sums_ref.shape
        size = deep - 8
        tall = tile // LANES
        total = jnp.zeros((tall, LANES), jnp.float32)
        group = math.gcd(lines, 8)
        for c in range(0, lines, group):
            ahead, behind = [], []
            for k in range(c, c + group):
                ids = ids_at(k)
                high = lax.shift_right_arithmetic(ids, 7)
                rest = ids & (LANES - 1)
                ahead.append(
                    jnp.where(high == lax.broadcasted_iota(jnp.int32, (tall, LANES), 0), 1.0, 0.0)
                )
                behind.append(
                    jnp.where(rest == lax.broadcasted_iota(jnp.int32, (LANES, LANES), 0), 1.0, 0.0)
                )
            total = total + lax.dot_general(
                jnp.concatenate(ahead, axis=1).astype(jnp.bfloat16),
                jnp.concatenate(behind, axis=1).astype(jnp.bfloat16),
                (((1,), (1,)), ((), ())),
                preferred_element_type=jnp.float32,
            )
        counts = size // LANES
        for k in range(shards):
            line = total[k * counts : (k + 1) * counts]
            if first:
                if counts < 8:
                    sums_ref[k, size:, :] = jnp.zeros((8, LANES), jnp.float32)
                sums_ref[k, size : size + counts, :] = line
            else:
                sums_ref[k, size : size + counts, :] += line

        block = math.gcd(math.gcd(span, 1024), 2 * size)
        piece = min(block, size)
        per = size // piece

        def step(b, carry):
            acc = pick(b * block, block, lines)
            for side in range(2):
                for k in range(block // piece):
                    index = (b + side * (span // block)) * (block // piece) + k
                    spot = pl.ds(pl.multiple_of(lax.rem(index, per) * piece, piece), piece)
                    value = acc[
                        k * piece : (k + 1) * piece, side * LANES : (side + 1) * LANES
                    ]
                    if first:
                        sums_ref[index // per, spot, :] = value
                    else:
                        sums_ref[index // per, spot, :] += value
            return carry

        if turns is None:
            lax.fori_loop(0, span // block, step, 0)
        else:
            for b, after in turns(span // block):
                step(b, 0)
                after()

    lines = rows // LANES
    cap_lines = cap // LANES
    block = math.gcd(cap, 1024)

    split(lambda c: place_ref[pl.ds(c, 1), :], lambda spot: wattrs_ref[spot, :], lines, half * cap)
    pl.semaphore_wait(barrier, wa_size - 1 + af_high)

    own_high, own_low = [], []
    for h in range(1, af_high):
        where = af_peer(lax.rem(af_top + h, af_high), af_low)
        own_high.append(
            (
                copy(fattrs_ref, inf_ref.at[2 * h], where),
                copy(fids_ref, idf_ref.at[2 * h], where),
            )
        )
    where = af_peer(af_top, 1 - af_low)
    own_low.append(
        (copy(fattrs_ref, inf_ref.at[1], where), copy(fids_ref, idf_ref.at[1], where))
    )
    for pair in own_high + own_low:
        for c in pair:
            c.start()

    sent = {}
    for i in range(half):
        q = lax.rem(wa + i, half)
        one = lax.rem(q - wa + wa_size, wa_size)
        two = lax.rem(one + half, wa_size)

        def fill_block(b, carry):
            acc = pick(q * cap + b * block, block, lines)
            spot = pl.ds(pl.multiple_of(b * block, block), block)
            send_ref[one, spot, :] = acc[:, :LANES].astype(jnp.bfloat16)
            send_ref[two, spot, :] = acc[:, LANES:].astype(jnp.bfloat16)
            return carry

        lax.fori_loop(0, cap // block, fill_block, 0)
        for d in (i + half, i):
            if d:
                to = lax.rem(wa + d, wa_size)
                sent[d] = (
                    copy(send_ref.at[d], inw_ref.at[d - 1], (to, af)),
                    copy(wids_ref.at[to], idw_ref.at[d - 1], (to, af)),
                )
                for c in sent[d]:
                    c.start()

    def scatter_near(order, sums_ref, near_ref, high, top, low, peer):
        return [
            copy(
                sums_ref.at[lax.rem(top + h, high) * 2 + 1 - low],
                near_ref.at[h],
                peer(top, 1 - low),
            )
            for h in order
        ]

    at_wa = (wa_high, wa_top, wa_low, wa_peer)
    at_af = (af_high, af_top, af_low, af_peer)
    folds = wa_high // 2
    order_f = [h % wa_high for j in range(1, folds + 1) for h in (j, j + folds)]
    order_w = list(range(1, af_high)) + [0]
    near_firm = scatter_near(order_f, fsum_ref, near_f, *at_wa)

    def firm_turns(count):
        out = []
        for j in range(count):
            some = near_firm[j * wa_high // count : (j + 1) * wa_high // count]
            out.append((lax.rem(wa_top + j + 1, count), lambda some=some: [c.start() for c in some]))
        return out

    base = af * ft

    def take_firm(ids_ref, attrs_ref, first, turns=None):
        pool(
            lambda c: ids_ref[pl.ds(c, 1), :] - base,
            lambda spot: attrs_ref[spot, :],
            lines, ft, fsum_ref, first, turns,
        )

    take_firm(fids_ref, fattrs_ref, True)
    forwards = []
    for h in range(1, af_high):
        for c in own_high[h - 1]:
            c.wait_recv()
        pair = (
            copy(inf_ref.at[2 * h], inf_ref.at[2 * h + 1], af_peer(af_top, 1 - af_low)),
            copy(idf_ref.at[2 * h], idf_ref.at[2 * h + 1], af_peer(af_top, 1 - af_low)),
        )
        for c in pair:
            c.start()
        forwards.append(pair)
    for c in own_low[0]:
        c.wait_recv()
    take_firm(idf_ref.at[1], inf_ref.at[1], False)
    for h in range(1, af_high):
        take_firm(idf_ref.at[2 * h], inf_ref.at[2 * h], False)
    for h in range(1, af_high):
        for c in forwards[h - 1]:
            c.wait_recv()
        take_firm(
            idf_ref.at[2 * h + 1], inf_ref.at[2 * h + 1], False,
            firm_turns if h == af_high - 1 else None,
        )

    def scatter_far(i, order, copies, out, sums_ref, near_ref, part_ref, far_ref, high, top, low, peer):
        h = order[i]
        copies[i].wait_recv()
        shard = lax.rem(top + h, high)
        part_ref[h] = sums_ref[shard * 2 + low] + near_ref[h]
        if h:
            out[h] = copy(part_ref.at[h], far_ref.at[h - 1], peer(shard, low))
            out[h].start()

    def scatter_end(copies, part_ref, far_ref, high):
        for h in range(1, high):
            copies[h].wait_recv()
            part_ref[0] += far_ref[h - 1]

    def spread_far(refs, high, top, low, peer):
        copies = [[] for _ in range(high)]
        mine = top * 2 + low
        for ref in refs:
            for h in range(1, high):
                copies[h].append(copy(ref.at[mine], ref.at[mine], peer(lax.rem(top + h, high), low)))
            copies[0].append(copy(ref.at[mine], ref.at[mine], peer(top, 1 - low)))
        for h in list(range(1, high)) + [0]:
            for c in copies[h]:
                c.start()
        return copies

    def spread_near(copies, refs, high, top, low, peer):
        out = []
        for h in range(1, high):
            for c in copies[h]:
                c.wait_recv()
            origin = lax.rem(top - h + high, high) * 2 + low
            for ref in refs:
                out.append(copy(ref.at[origin], ref.at[origin], peer(top, 1 - low)))
                out[-1].start()
        return out


    def take_worker(d, first=False):
        if d:
            for c in sent[d]:
                c.wait_recv()
            ids, attrs = idw_ref.at[d - 1], inw_ref.at[d - 1]
        else:
            ids, attrs = wids_ref.at[wa], send_ref.at[0]
        pool(
            lambda c: ids[pl.ds(c, 1), :],
            lambda spot: attrs[spot, :],
            cap_lines, wt, wsum_ref, first,
        )

    order = [0]
    for i in range(half):
        order += [d for d in (i + half, i) if d]
    far_firm, far_worker, step = {}, {}, 0
    for n, d in enumerate(order):
        take_worker(d, n == 0)
        if n >= 2 and n % 2 == 0 and step < wa_high - 1:
            scatter_far(step, order_f, near_firm, far_firm, fsum_ref, near_f, part_f, far_f, *at_wa)
            step += 1

    near_worker = scatter_near(order_w, wsum_ref, near_w, *at_af)
    for c in near_worker:
        c.start()
    for i in range(af_high):
        scatter_far(i, order_w, near_worker, far_worker, wsum_ref, near_w, part_w, far_w, *at_af)
    for i in range(step, wa_high):
        scatter_far(i, order_f, near_firm, far_firm, fsum_ref, near_f, part_f, far_f, *at_wa)

    def finish_means(part_ref, size, emit):
        def step(r, carry):
            tally = upright(part_ref[0, pl.ds(size + r, 1), :])
            spot = pl.ds(pl.multiple_of(r * LANES, LANES), LANES)
            means = part_ref[0, spot, :] / jnp.maximum(tally, 1.0)
            top = means.astype(jnp.bfloat16)
            emit(spot, top, (means - top.astype(jnp.float32)).astype(jnp.bfloat16))
            return carry

        lax.fori_loop(0, size // LANES, step, 0)

    def emit_worker(spot, means, rest):
        wtop_ref[spot, :] = means
        wrest_ref[spot, :] = rest
        proj_ref[af, spot, :] = jnp.dot(
            means, affinity_ref[...], preferred_element_type=jnp.float32
        ).astype(jnp.bfloat16)

    def emit_firm(spot, means, rest):
        frest_ref[spot, :] = rest
        frows_ref[wa, spot, :] = means

    scatter_end(far_firm, part_f, far_f, wa_high)
    finish_means(part_f, whole_f, emit_firm)
    ftally_ref[wa] = part_f[0, whole_f:, :]
    firm_far = spread_far((frows_ref, ftally_ref), *at_wa)
    scatter_end(far_worker, part_w, far_w, af_high)
    finish_means(part_w, whole_w, emit_worker)
    wtally_ref[af] = part_w[0, whole_w:, :]
    worker_far = spread_far((proj_ref, wtally_ref), *at_af)
    worker_near = spread_near(worker_far, (proj_ref, wtally_ref), *at_af)
    firm_near = spread_near(firm_far, (frows_ref, ftally_ref), *at_wa)
    for c in worker_far[0] + firm_far[0] + worker_near + firm_near:
        c.wait_recv()
    done = [c for pair in own_high + own_low + forwards + list(sent.values()) for c in pair]
    done += near_firm + near_worker + worker_near + firm_near
    done += list(far_firm.values()) + list(far_worker.values())
    done += [c for group in worker_far + firm_far for c in group]
    for c in done:
        c.wait_send()


def route(place, worker_attrs, sent_ids, firm_ids, firm_attrs, affinity, cap):
    wa_size, af_size = lax.axis_size("wa"), lax.axis_size("af")
    rows = worker_attrs.shape[0]
    wt, ft = W // wa_size, F // af_size
    sw, sf = wt // af_size, ft // wa_size
    lines = rows // LANES
    wa_high, af_high = wa_size // 2, af_size // 2
    vmem = pl.BlockSpec(memory_space=pltpu.VMEM)
    f32, bf16, i32 = jnp.float32, jnp.bfloat16, jnp.int32
    copies = 4 * af_high + 2 * (wa_size - 1) + 4 * (wa_high + af_high)
    copies += 4 * (wa_high + af_high)
    return pl.pallas_call(
        functools.partial(route_kernel, wa_size, af_size, cap),
        out_shape=(
            jax.ShapeDtypeStruct((sw, LANES), bf16),
            jax.ShapeDtypeStruct((sw, LANES), bf16),
            jax.ShapeDtypeStruct((sf, LANES), bf16),
            jax.ShapeDtypeStruct((af_size, sw, LANES), bf16),
            jax.ShapeDtypeStruct((wa_size, sf, LANES), bf16),
            jax.ShapeDtypeStruct((af_size, 8, LANES), f32),
            jax.ShapeDtypeStruct((wa_size, 8, LANES), f32),
        ),
        in_specs=[vmem] * 6,
        out_specs=(vmem,) * 7,
        scratch_shapes=[
            pltpu.VMEM((rows, 2 * LANES), bf16),
            pltpu.VMEM((lines, LANES), i32),
            pltpu.VMEM((wa_size, cap, LANES), bf16),
            pltpu.VMEM((wa_size - 1, cap, LANES), bf16),
            pltpu.VMEM((wa_size - 1, cap // LANES, LANES), i32),
            pltpu.VMEM((af_size, rows, LANES), bf16),
            pltpu.VMEM((af_size, lines, LANES), i32),
            pltpu.VMEM((af_size, sw + 8, LANES), f32),
            pltpu.VMEM((wa_size, sf + 8, LANES), f32),
            pltpu.VMEM((af_high, sw + 8, LANES), f32),
            pltpu.VMEM((af_high, sw + 8, LANES), f32),
            pltpu.VMEM((max(af_high - 1, 1), sw + 8, LANES), f32),
            pltpu.VMEM((wa_high, sf + 8, LANES), f32),
            pltpu.VMEM((wa_high, sf + 8, LANES), f32),
            pltpu.VMEM((max(wa_high - 1, 1), sf + 8, LANES), f32),
            pltpu.SemaphoreType.DMA((copies,)),
            pltpu.SemaphoreType.DMA((copies,)),
        ],
        compiler_params=pltpu.CompilerParams(
            collective_id=1, has_side_effects=True, vmem_limit_bytes=VMEM_BYTES
        ),
        name="route",
    )(
        place.reshape(lines, LANES),
        worker_attrs,
        sent_ids.reshape(wa_size, cap // LANES, LANES),
        firm_ids.reshape(lines, LANES),
        firm_attrs,
        affinity,
    )


def pack_records(type_ids, tile, groups, capacity):
    rows = type_ids.shape[0]
    owner = type_ids // tile
    local = type_ids - owner * tile
    grid = owner.reshape(rows // LANES, LANES)
    hits = (grid[None] == jnp.arange(groups, dtype=jnp.int32)[:, None, None])
    ramp = jnp.arange(LANES, dtype=jnp.int32)
    upper = (ramp[:, None] <= ramp[None, :]).astype(jnp.bfloat16)
    within = jnp.dot(hits.astype(jnp.bfloat16), upper, preferred_element_type=jnp.float32)
    lines = within[:, :, -1]
    line = jnp.arange(rows // LANES, dtype=jnp.int32)
    before = jnp.sum(
        jnp.where(line[None, :, None] < line[None, None, :], lines[:, :, None], 0.0), axis=1
    )
    rank = jnp.sum(jnp.where(hits, within - 1.0 + before[:, :, None], 0.0), axis=0)
    place = (grid * capacity + rank.astype(jnp.int32)).reshape(rows)
    high, lowd = local // 64, local % 64
    filled = jnp.full((groups * capacity,), tile, jnp.int32)
    chosen = place_ids(place, jnp.stack([high, lowd, jnp.ones_like(high)]), groups, capacity)
    sent_ids = jnp.where(chosen[2] > 0.5, (chosen[0] * 64.0 + chosen[1]).astype(jnp.int32), filled)
    return (place, sent_ids.reshape(groups, capacity))


def place_ids(place, digits, groups, capacity):
    slots = groups * capacity
    high, low = place // LANES, place % LANES
    ahead = (high[None, :] == jnp.arange(slots // LANES, dtype=jnp.int32)[:, None])
    behind = (low[None, :] == jnp.arange(LANES, dtype=jnp.int32)[:, None]).astype(jnp.bfloat16)
    out = []
    for d in range(digits.shape[0]):
        left = jnp.where(ahead, digits[d][None, :].astype(jnp.bfloat16), jnp.bfloat16(0))
        out.append(
            lax.dot_general(left, behind, (((1,), (1,)), ((), ())), preferred_element_type=jnp.float32)
        )
    return jnp.stack(out).reshape(digits.shape[0], slots)


def joined(value, axis, combine):
    everything = jax.tree.map(lambda part: lax.all_gather(part, axis), value)
    initial = jax.tree.map(lambda part: part[0], everything)

    def step(k, so_far):
        return combine(so_far, jax.tree.map(lambda part: part[k], everything))

    return lax.fori_loop(1, lax.axis_size(axis), step, initial)


def merge_pair(left, right):
    peak = jnp.maximum(left[0], right[0])
    return (peak, left[1] * jnp.exp(left[0] - peak) + right[1] * jnp.exp(right[0] - peak))


def log_sweeps(projected, firm_rows, log_worker, log_firm):
    worker_tile, firm_tile = projected.shape[0], firm_rows.shape[0]
    height = math.gcd(worker_tile, 512)
    blocks = worker_tile // height

    def surplus(index):
        rows_block = lax.dynamic_slice_in_dim(projected, index * height, height, 0)
        return jnp.dot(rows_block, firm_rows.T, preferred_element_type=jnp.float32)

    def sweep(rounds, carry):
        firm_potential = carry[1]

        def row_stats(index):
            scores = surplus(index) + firm_potential[None, :]
            peak = jnp.max(scores, axis=1)
            return (peak, jnp.sum(jnp.exp(scores - peak[:, None]), axis=1))

        peak, total = lax.map(row_stats, jnp.arange(blocks, dtype=jnp.int32))
        peak, total = joined((peak.reshape(-1), total.reshape(-1)), "af", merge_pair)
        worker_potential = log_worker - (peak + jnp.log(total))

        def col_step(carry, inputs):
            peak, total = carry
            index, shift_block = inputs
            scores = surplus(index) + shift_block[:, None]
            new_peak = jnp.maximum(peak, jnp.max(scores, axis=0))
            total = total * jnp.exp(peak - new_peak) + jnp.sum(
                jnp.exp(scores - new_peak[None, :]), axis=0
            )
            return ((new_peak, total), None)

        start = (
            jnp.full((firm_tile,), -jnp.inf, jnp.float32),
            jnp.zeros((firm_tile,), jnp.float32),
        )
        (peak, total), _ = lax.scan(
            col_step,
            start,
            (jnp.arange(blocks, dtype=jnp.int32), worker_potential.reshape(blocks, height)),
        )
        peak, total = joined((peak, total), "wa", merge_pair)
        return (worker_potential, log_firm - (peak + jnp.log(total)))

    start = (jnp.zeros((worker_tile,), jnp.float32), jnp.zeros((firm_tile,), jnp.float32))
    return lax.fori_loop(0, ITERS, sweep, start)


TINY = 4e-28
LEAST = 1e-25
MOST = 1e30


def sweep_kernel(
    wa_size, af_size, records, proj_ref, rows_ref, wtally_ref, ftally_ref, wtop_ref, wrest_ref, frest_ref,
    wpot_ref, fpot_ref, bad_ref, wtops_ref, wrests_ref, frests_ref,
    e_ref, s_ref, firm_ref, v_ref, u_ref, vb_ref, col_ref, wplus_ref, fplus_ref,
    in_p, in_w, in_h, in_f, in_a, in_b, send_sem, recv_sem,
):
    wa, af = lax.axis_index("wa"), lax.axis_index("af")
    wt, ft = proj_ref.shape[0], rows_ref.shape[0]
    wr, fr = wt // LANES, ft // LANES
    wa_high, af_high = wa_size // 2, af_size // 2
    wa_top, wa_low = wa // 2, lax.rem(wa, 2)
    af_top, af_low = af // 2, lax.rem(af, 2)
    worker_all, firm_all = float(records + W), float(records + F)

    barrier = pltpu.get_barrier_semaphore()
    for d in range(1, af_size):
        pl.semaphore_signal(
            barrier, inc=1, device_id=(wa, lax.rem(af + d, af_size)), device_id_type=MESH
        )
    for d in range(1, wa_size):
        pl.semaphore_signal(
            barrier, inc=1, device_id=(lax.rem(wa + d, wa_size), af), device_id_type=MESH
        )

    eye = lax.broadcasted_iota(jnp.int32, (LANES, LANES), 0) == lax.broadcasted_iota(
        jnp.int32, (LANES, LANES), 1
    )

    def lay(column):
        return jnp.sum(jnp.where(eye, column, 0.0), axis=0, keepdims=True)

    def halves(rows):
        row = jnp.concatenate(rows, axis=1)
        top = row.astype(jnp.bfloat16)
        rest = (row - top.astype(jnp.float32)).astype(jnp.bfloat16)
        return jnp.concatenate([top, rest, jnp.zeros((6, row.shape[1]), jnp.bfloat16)], axis=0)

    used = []

    def push(ref, index, peer):
        used.append(
            pltpu.make_async_remote_copy(
                src_ref=ref.at[index],
                dst_ref=ref.at[index],
                send_sem=send_sem.at[len(used)],
                recv_sem=recv_sem.at[len(used)],
                device_id=peer,
                device_id_type=MESH,
            )
        )
        used[-1].start()
        return used[-1]

    def exchange(inbox, along_af):
        size, me = (af_size, af) if along_af else (wa_size, wa)
        copies = []
        for d in sorted(range(1, size), key=lambda d: abs(2 * d - size)):
            peer = (wa, lax.rem(af + d, size)) if along_af else (lax.rem(wa + d, size), af)
            copies.append(push(inbox, me, peer))
        return copies

    def arrive(copies):
        for copy in copies:
            copy.wait_recv()

    hr, hf = wr // 2, fr // 2

    def fill(p, start, stop):
        def block(b, carry):
            spot = pl.ds(pl.multiple_of(p * hr * LANES + b * 256, 256), 256)
            peak = jnp.full((256, LANES), -jnp.inf, jnp.float32)
            for c in range(ft // 512):
                scores = jnp.dot(
                    proj_ref[spot, :],
                    firm_ref[:, c * 512 : (c + 1) * 512],
                    preferred_element_type=jnp.float32,
                )
                s_ref[:, c * 512 : (c + 1) * 512] = scores
                for k in range(4):
                    peak = jnp.maximum(peak, scores[:, k * LANES : (k + 1) * LANES])
            peak = jnp.max(peak, axis=1, keepdims=True)
            shift = jnp.broadcast_to(peak, (256, LANES))
            acc = jnp.zeros((256, LANES), jnp.float32)
            for c in range(fr):
                grown = jnp.exp(s_ref[:, c * LANES : (c + 1) * LANES] - shift)
                e_ref[spot, c * LANES : (c + 1) * LANES] = grown.astype(jnp.bfloat16)
                acc = acc + grown
            total = jnp.sum(acc, axis=1, keepdims=True)
            for k in range(2):
                part = slice(k * LANES, (k + 1) * LANES)
                in_p[p, af, pl.ds(b * 2 + k, 1), :] = lay(total[part])
                in_p[p, af, pl.ds(hr + b * 2 + k, 1), :] = lay(peak[part])
            return carry

        lax.fori_loop(start, stop, block, 0)

    lead = hf // 4
    group = math.gcd(hf - lead, 4)

    def row_pass(p, g):
        first, last = g * hf, (g + 1) * hf
        spread = halves([v_ref[c : c + 1, :] for c in range(first, first + lead)])

        def block(b, carry):
            spot = pl.ds(pl.multiple_of(p * hr * LANES + b * 256, 256), 256)
            near = lax.dot_general(
                spread,
                e_ref[spot, first * LANES : (first + lead) * LANES],
                (((1,), (1,)), ((), ())),
                preferred_element_type=jnp.float32,
            )
            near = near[0:1] + near[1:2]
            for k in range(2):
                part = pl.ds(
                    pl.multiple_of((p * hr + k) * LANES + b * 256, LANES), LANES
                )
                acc = jnp.zeros((LANES, LANES), jnp.float32)
                for c in range(first + lead, last, group):
                    terms = [
                        e_ref[part, i * LANES : (i + 1) * LANES] * vb_ref[i : i + 1, :]
                        for i in range(c, c + group)
                    ]
                    while len(terms) > 1:
                        terms = [x + y for x, y in zip(terms[::2], terms[1::2])]
                    acc = acc + terms[0].astype(jnp.float32)
                row = near[:, k * LANES : (k + 1) * LANES] + lay(
                    jnp.sum(acc, axis=1, keepdims=True)
                )
                line = pl.ds(p * hr + b * 2 + k, 1)
                if g:
                    row = row + wpot_ref[line, :]
                wpot_ref[line, :] = row
            return carry

        lax.fori_loop(0, hr // 2, block, 0)

    def col_pass(p, g):
        deep = hr * LANES
        high = math.gcd(deep, 1024)
        lines = high // LANES
        span = slice(g * hf * LANES, (g + 1) * hf * LANES)

        def block(b, acc):
            spot = pl.ds(pl.multiple_of(p * deep + b * high, high), high)
            lhs = halves([u_ref[pl.ds(p * hr + b * lines + k, 1), :] for k in range(lines)])
            return acc + jnp.dot(lhs, e_ref[spot, span], preferred_element_type=jnp.float32)

        start = jnp.zeros((8, hf * LANES), jnp.float32) if p == 0 else col_ref[g]
        acc = lax.fori_loop(0, deep // high, block, start)
        if p == 0:
            col_ref[g] = acc
            return None
        total = acc[0:1] + acc[1:2]
        return [total[:, c * LANES : (c + 1) * LANES] for c in range(hf)]

    def least(value):
        return jnp.min(value, axis=0, keepdims=True)

    def most(value):
        return jnp.max(value, axis=0, keepdims=True)

    in_a[wa] = jnp.zeros((16, LANES), jnp.float32)
    in_b[af] = jnp.zeros((16, LANES), jnp.float32)
    for ref, tally_ref, per in (
        (wplus_ref, wtally_ref, wr // af_size),
        (fplus_ref, ftally_ref, fr // wa_size),
    ):
        for k in range(tally_ref.shape[0]):
            ref[k * per : (k + 1) * per, :] = tally_ref[k, :per, :] + 1.0
    for c in range(fr):
        spot = slice(c * LANES, (c + 1) * LANES)
        firm_ref[:, spot] = rows_ref[spot, :].astype(jnp.float32).T.astype(jnp.bfloat16)
    wtops_ref[af] = wtop_ref[...]
    wrests_ref[af] = wrest_ref[...]
    frests_ref[wa] = frest_ref[...]
    steps = hr // 2
    fill(0, 0, steps // 4)
    pl.semaphore_wait(barrier, af_size + wa_size - 2)
    worker_far = [
        push(ref, af, (wa, lax.rem(af_top + h, af_high) * 2 + af_low))
        for h in range(1, af_high)
        for ref in (wtops_ref, wrests_ref)
    ]
    firm_far = [
        push(frests_ref, wa, (lax.rem(wa_top + h, wa_high) * 2 + wa_low, af))
        for h in range(1, wa_high)
    ]
    beside_w, beside_f = (wa, af_top * 2 + 1 - af_low), (wa_top * 2 + 1 - wa_low, af)
    near = [push(frests_ref, wa, beside_f)]
    near += [push(ref, af, beside_w) for ref in (wtops_ref, wrests_ref)]
    fill(0, steps // 4, steps)
    moving = [exchange(in_p.at[0], True)]
    fill(1, 0, steps // 2)
    for h in range(1, wa_high):
        firm_far[h - 1].wait_recv()
        origin = lax.rem(wa_top - h + wa_high, wa_high) * 2 + wa_low
        near.append(push(frests_ref, origin, beside_f))
    for h in range(1, af_high):
        origin = lax.rem(af_top - h + af_high, af_high) * 2 + af_low
        for i, ref in enumerate((wtops_ref, wrests_ref)):
            worker_far[2 * (h - 1) + i].wait_recv()
            near.append(push(ref, origin, beside_w))
    fill(1, steps // 2, steps)
    moving.append(exchange(in_p.at[1], True))
    scale, top = [None, None], [None, None]
    for turn in range(ITERS):
        final = turn == ITERS - 1
        stats = []
        for p in range(2):
            arrive(moving[p])
            total = jnp.zeros((hr, LANES), jnp.float32)
            if turn == 0:
                peaks = [in_p[p, k, hr:] for k in range(af_size)]
                top[p] = functools.reduce(jnp.maximum, peaks)
                scale[p] = jnp.exp(in_p[p, af, hr:] - top[p])
                for k in range(af_size):
                    total = total + in_p[p, k, :hr] * jnp.exp(peaks[k] - top[p])
            else:
                for k in range(af_size):
                    total = total + in_w[(turn - 1) * 2 + p, k]
            here = slice(p * hr, (p + 1) * hr)
            u = (wplus_ref[here, :] / worker_all) / total
            u_ref[here, :] = u * scale[p]
            stats.append((least(total), most(total), most(u), least(u)))
            if final:
                log_a = jnp.log(wplus_ref[here, :]) - math.log(worker_all)
                wpot_ref[here, :] = log_a - (top[p] + jnp.log(total))
            if p == 0:
                col_pass(0, 0)
                col_pass(0, 1)
        one, two = stats
        in_a[wa, turn : turn + 1, :] = jnp.minimum(one[0], two[0])
        in_a[wa, 3 + turn : 4 + turn, :] = jnp.maximum(one[1], two[1])
        in_a[wa, 6 + turn : 7 + turn, :] = jnp.maximum(one[2], two[2])
        in_a[wa, 9 + turn : 10 + turn, :] = jnp.minimum(one[3], two[3])
        moving = []
        for g in range(2):
            parts = col_pass(1, g)
            if final:
                for c in range(hf):
                    in_f[g, wa, c : c + 1, :] = parts[c]
                moving.append(exchange(in_f.at[g], False))
            else:
                in_h[turn * 2 + g, wa] = jnp.concatenate(parts, axis=0).astype(in_h.dtype)
                moving.append(exchange(in_h.at[turn * 2 + g], False))
        if final:
            verdict_a = exchange(in_a, False)
        stats = []
        for g in range(2):
            arrive(moving[g])
            total = jnp.zeros((hf, LANES), jnp.float32)
            for k in range(wa_size):
                total = total + (
                    in_f[g, k] if final else in_h[turn * 2 + g, k].astype(jnp.float32)
                )
            here = slice(g * hf, (g + 1) * hf)
            if final:
                log_b = jnp.log(fplus_ref[here, :]) - math.log(firm_all)
                fpot_ref[here, :] = log_b - jnp.log(total)
                stats.append((least(total), most(total)))
            else:
                v = (fplus_ref[here, :] / firm_all) / total
                v_ref[here, :] = v
                vb_ref[here, :] = v.astype(vb_ref.dtype)
                stats.append((least(total), most(total), most(v)))
                if g == 0:
                    row_pass(0, 0)
                    row_pass(1, 0)
                else:
                    moving = []
                    for p in range(2):
                        row_pass(p, 1)
                        spot = slice(p * hr, (p + 1) * hr)
                        in_w[turn * 2 + p, af] = wpot_ref[spot, :] * scale[p]
                        moving.append(exchange(in_w.at[turn * 2 + p], True))
        one, two = stats
        in_b[af, turn : turn + 1, :] = jnp.minimum(one[0], two[0])
        in_b[af, 3 + turn : 4 + turn, :] = jnp.maximum(one[1], two[1])
        if not final:
            in_b[af, 7 + turn : 8 + turn, :] = jnp.maximum(one[2], two[2])
    in_b[af, 6:7, :] = jnp.ones((1, LANES), jnp.float32)
    verdict_b = exchange(in_b, True)
    arrive(verdict_a)
    low_a = functools.reduce(jnp.minimum, [in_a[k] for k in range(wa_size)])
    high_a = functools.reduce(jnp.maximum, [in_a[k] for k in range(wa_size)])
    low_a = jnp.broadcast_to(jnp.min(low_a, axis=1, keepdims=True), (16, LANES))
    high_a = jnp.broadcast_to(jnp.max(high_a, axis=1, keepdims=True), (16, LANES))
    arrive(verdict_b)
    low_b = functools.reduce(jnp.minimum, [in_b[k] for k in range(af_size)])
    high_b = functools.reduce(jnp.maximum, [in_b[k] for k in range(af_size)])
    low_b = jnp.broadcast_to(jnp.min(low_b, axis=1, keepdims=True), (16, LANES))
    high_b = jnp.broadcast_to(jnp.max(high_b, axis=1, keepdims=True), (16, LANES))
    good = jnp.ones((1, LANES), jnp.float32)
    for turn in range(ITERS):
        row = slice(turn, turn + 1)
        three = slice(3 + turn, 4 + turn)
        six = slice(6 + turn, 7 + turn)
        nine = slice(9 + turn, 10 + turn)
        for ok in (
            low_a[row] > LEAST,
            high_a[three] < MOST,
            high_b[six] * TINY <= low_a[row],
            low_b[row] > LEAST,
            high_b[three] < MOST,
            high_a[six] * TINY <= low_b[row],
            low_a[nine] >= 1e-35,
        ):
            good = jnp.where(ok, good, 0.0)
    bad_ref[0, 0] = 1.0 - jnp.min(good)
    arrive(near)
    for copy in used:
        copy.wait_send()


def fast_sweeps(projected, firm_rows, worker_tally, firm_tally, worker_top, worker_rest, firm_rest, records):
    wa_size, af_size = lax.axis_size("wa"), lax.axis_size("af")
    wt, ft = projected.shape[0], firm_rows.shape[0]
    wr, fr = wt // LANES, ft // LANES
    vmem = pl.BlockSpec(memory_space=pltpu.VMEM)
    f32 = jnp.float32
    copies = (2 * ITERS + 2) * (af_size + wa_size - 2) + af_size
    hr, hf = wr // 2, fr // 2
    kind = jnp.bfloat16 if hf % 16 == 0 else f32
    return pl.pallas_call(
        functools.partial(sweep_kernel, wa_size, af_size, records),
        out_shape=(
            jax.ShapeDtypeStruct((wr, LANES), f32),
            jax.ShapeDtypeStruct((fr, LANES), f32),
            jax.ShapeDtypeStruct((1, 1), f32),
            jax.ShapeDtypeStruct((af_size,) + worker_top.shape, jnp.bfloat16),
            jax.ShapeDtypeStruct((af_size,) + worker_top.shape, jnp.bfloat16),
            jax.ShapeDtypeStruct((wa_size,) + firm_rest.shape, jnp.bfloat16),
        ),
        in_specs=[vmem] * 7,
        out_specs=(vmem, vmem, pl.BlockSpec(memory_space=pltpu.SMEM), vmem, vmem, vmem),
        scratch_shapes=[
            pltpu.VMEM((wt, ft), jnp.bfloat16),
            pltpu.VMEM((256, ft), f32),
            pltpu.VMEM((LANES, ft), jnp.bfloat16),
            pltpu.VMEM((fr, LANES), f32),
            pltpu.VMEM((wr, LANES), f32),
            pltpu.VMEM((fr, LANES), jnp.bfloat16 if fr % 32 == 0 else f32),
            pltpu.VMEM((2, 8, hf * LANES), f32),
            pltpu.VMEM((wr, LANES), f32),
            pltpu.VMEM((fr, LANES), f32),
            pltpu.VMEM((2, af_size, 2 * hr, LANES), f32),
            pltpu.VMEM(((ITERS - 1) * 2, af_size, hr, LANES), f32),
            pltpu.VMEM(((ITERS - 1) * 2, wa_size, hf, LANES), kind),
            pltpu.VMEM((2, wa_size, hf, LANES), f32),
            pltpu.VMEM((wa_size, 16, LANES), f32),
            pltpu.VMEM((af_size, 16, LANES), f32),
            pltpu.SemaphoreType.DMA((copies,)),
            pltpu.SemaphoreType.DMA((copies,)),
        ],
        compiler_params=pltpu.CompilerParams(
            collective_id=0, has_side_effects=True, vmem_limit_bytes=VMEM_BYTES
        ),
        name="sweeps",
    )(projected, firm_rows, worker_tally, firm_tally, worker_top, worker_rest, firm_rest)


def body(worker_ids, worker_attrs, firm_ids, firm_attrs, affinity):
    rows = worker_ids.shape[0]
    wa_count = lax.axis_size("wa")
    af_count = lax.axis_size("af")
    worker_tile = W // wa_count
    firm_tile = F // af_count
    records_all = rows * wa_count * af_count
    cap = 2 * rows // wa_count
    place, sent_ids = pack_records(worker_ids, worker_tile, wa_count, cap)
    worker_top, worker_rest, firm_rest, projected, firm_rows, worker_tally, firm_tally = route(
        place, worker_attrs, sent_ids, firm_ids, firm_attrs, affinity, cap
    )
    projected = projected.reshape(worker_tile, LANES)
    firm_rows = firm_rows.reshape(firm_tile, LANES)
    worker_potential, firm_potential, bad, tops, rests, firm_rests = fast_sweeps(
        projected, firm_rows, worker_tally, firm_tally,
        worker_top, worker_rest, firm_rest, records_all,
    )

    def whole(top, rest):
        return top.reshape(-1, LANES).astype(jnp.float32) + rest.reshape(-1, LANES).astype(
            jnp.float32
        )

    worker_means = whole(tops, rests)
    firm_means = whole(firm_rows, firm_rests)

    def careful():
        worker_each = worker_tally[:, : worker_top.shape[0] // LANES].reshape(worker_tile)
        firm_each = firm_tally[:, : firm_rest.shape[0] // LANES].reshape(firm_tile)
        log_worker = jnp.log(worker_each + 1.0) - jnp.log(jnp.float32(records_all + W))
        log_firm = jnp.log(firm_each + 1.0) - jnp.log(jnp.float32(records_all + F))
        return log_sweeps(projected, firm_rows, log_worker, log_firm)

    worker_potential, firm_potential = lax.cond(
        bad[0, 0] > 0.5,
        careful,
        lambda: (worker_potential.reshape(-1), firm_potential.reshape(-1)),
    )
    return (
        worker_means,
        firm_means,
        worker_potential,
        firm_potential,
    )


def solution(mesh):
    placed = (P(("wa", "af")), P(("wa", "af"), None), P(("wa", "af")), P(("wa", "af"), None), P())
    return jax.shard_map(
        body,
        mesh=mesh,
        in_specs=placed,
        out_specs=(P("wa", None), P("af", None), P("wa"), P("af")),
        check_vma=False,
    )
```
